32 devices in a mesh: groups: 2 (over y), seq: 4 (over z), exp: 4 (over x, core).
Axes of the slice: x: 2, y: 2, z: 4, core: 2. Of those that a mesh axis runs over, the one named last changes fastest.
Arguments:
- residual: bfloat16 [2048, 2048], P(('groups', 'seq', 'exp')), parts along dimension 0, may hold values from -6 to 6
- mixer_input: bfloat16 [2, 2048, 4096], P(None, ('groups', 'seq'), 'exp'), parts along dimension 1, may hold values from -6 to 6
- step_raw: bfloat16 [2048, 4096], P(('groups', 'seq'), 'exp'), parts along dimension 0, may hold values from -3 to 1
- state_maps: bfloat16 [2, 16, 2048], P(None, None, ('groups', 'seq')), parts along dimension 2, may hold values from -2 to 2
- decay_rate: float32 [16, 4096], P(None, 'exp'), may hold values from 9.765625e-05 to 0.04
- skip_gain: float32 [4096], P('exp'), may hold values from 0.5 to 1.5
- out_weight: bfloat16 [4096, 2048], P('exp', 'seq'), may hold values from -0.09375 to 0.09375
- norm_gain: float32 [2048], replicated, may hold values from 0.1 to 1.9
- router_weight: bfloat16 [2048, 4], replicated, may hold values from -0.125 to 0.125
- expert_ids: int32 [2048, 2], P(('groups', 'seq', 'exp')), parts along dimension 0, may hold values from 0 to 3, all different within a row; in each aligned block of 64 rows (0 to 63, 64 to 127, ...) at most 42 rows name the same one
- gate_weight: bfloat16 [4, 2048, 7168], P('exp', None, 'seq'), may hold values from -0.125 to 0.125
- up_weight: bfloat16 [4, 2048, 7168], P('exp', None, 'seq'), may hold values from -0.125 to 0.125
- down_weight: bfloat16 [4, 7168, 2048], P('exp', 'seq'), may hold values from -0.0625 to 0.0625
Outputs:
- layer_out: bfloat16 [2048, 2048], P(('groups', 'seq', 'exp')), parts along dimension 0
The draws below stay inside these ranges and needn't reach their ends.
There are 2 independent parts, one for each index of `groups`. The reference program is written for one: setup_inputs(seed, part) draws one part's arguments, and reference() takes and returns one part's arrays. A program takes and returns all parts, laid end to end along the dimension named above; an argument that names none is the same for every part. Nothing has to cross between parts.
Inputs may be any that keep to these rules, and one draw needn't show every extreme that they name: `expert_ids`: each row names two different experts; within each aligned block of 64 rows (the rows of one device) no expert is named by more than 42 rows.
All inputs are finite; a program needn't handle non-finite values.
Results may differ from the reference program's by a relative error of at most 0.0061.
Values may be sent and summed in bfloat16 or wider, within the bound.
No kernel may reach another device: no remote copies, remote signals or barrier semaphores. Data moves between devices by JAX's collectives and lax.ppermute only.
A program may use at most 256 MiB of HBM per device.

```python
import math
import jax
import jax.numpy as jnp
import numpy as np
from jax import lax

D = 2048
INNER = 4096
NSTATE = 16
FF = 7168
TOPK = 2
HALF = 128
EXPERTS = 4
SEQ_DEV = 256
LENGTH = 1024
TOK_DEV = 64
CAP = 42
N_SEQ = 4


def levels(rng, dims, pieces, smallest, top_value):
    gain, own = 1.0, jax.random.fold_in(rng, 6)
    for dim, shards_of in pieces:
        steps = jnp.exp(jax.random.uniform(jax.random.fold_in(own, dim), (shards_of,), jnp.float32, smallest / len(pieces), top_value / len(pieces)))
        gain = gain * jnp.repeat(steps, dims[dim] // shards_of).reshape([-1 if axis == dim else 1 for axis in range(len(dims))])
    return gain


def assign_block(stream_key, own, number, rows, amount, top, reach, skew):
    sequence = jax.random.permutation(stream_key, amount)
    packed, usual = load_shares(amount, rows * top, reach, skew, True), load_shares(amount, rows * top, reach, skew, False)
    places = jnp.arange(amount)

    def named(lengths, turn):
        used = int((lengths > 0).sum())
        fixed = max(1, used // 4)
        moved = fixed + (places - fixed + turn * (used - fixed)) % max(1, amount - fixed)
        return jnp.zeros((amount,), jnp.int32).at[sequence[jnp.where(places < fixed, places, moved)]].set(jnp.asarray(lengths, jnp.int32))

    lengths = jnp.where(number % 4 == 0, named(packed, number // 4), named(usual, number - number // 4 - 1))
    mixed = jax.random.permutation(jax.random.fold_in(own, 3), amount)
    giver, sink = mixed[0:amount // 2 * 2:2], mixed[1:amount // 2 * 2:2]
    room = jnp.minimum(lengths[giver] - 1, reach - lengths[sink]) // 2
    room = jnp.where((giver == sequence[0]) | (sink == sequence[0]) | (lengths[sink] == 0), 0, jnp.maximum(room, 0))
    moved = jax.random.randint(jax.random.fold_in(own, 4), (amount // 2,), 0, 1 << 20) % (room + 1)
    lengths = lengths.at[giver].add(-moved).at[sink].add(moved)
    items = jnp.searchsorted(jnp.cumsum(lengths), jnp.arange(rows * top), side="right").astype(jnp.int32)
    grid = items.reshape(top, rows).T
    grid = grid[jax.random.permutation(jax.random.fold_in(own, 1), rows)]
    turn = jax.random.randint(jax.random.fold_in(own, 2), (rows, 1), 0, top)
    return jnp.take_along_axis(grid, (jnp.arange(top)[None, :] + turn) % top, axis=1)


def load_shares(amount, total, bound, slope, full):
    portions = [(1 << 20) // math.isqrt(rank ** slope) + 1 for rank in range(1, amount + 1)]
    largest = bound if full else min(bound, max(-(-total // amount), total * portions[0] // sum(portions)))
    least = 1 if total - largest >= amount - 1 else 0
    holding, rest = [largest] + [least] * (amount - 1), total - largest - least * (amount - 1)
    while rest > 0:
        free = [i for i in range(1, amount) if holding[i] < largest] or [i for i in range(1, amount) if holding[i] < bound]
        mass, budget = sum([portions[i] for i in free]), rest
        for i in free:
            addition = min(bound - holding[i], max(1, budget * portions[i] // mass), rest)
            holding[i] = holding[i] + addition
            rest = rest - addition
    return np.array(holding)


def bell_draw(stream_key, extent, spread, most, cuts=(), kind=jnp.bfloat16):
    entries = spread * jax.random.normal(stream_key, extent, jnp.float32)
    if cuts:
        entries = entries * levels(stream_key, extent, cuts, -0.22, 0.18)
    return jnp.clip(entries, -most, most).astype(kind)


def setup_inputs(seed: int = 0, part: int = 0) -> dict:
    seeds = jax.random.split(jax.random.key(seed), 14)
    own_keys = jax.random.split(jax.random.fold_in(seeds[13], part), 14)
    residual = bell_draw(own_keys[0], (LENGTH, D), 1.0, 6.0, ((0, 16),))
    mixer_input = bell_draw(own_keys[1], (2, LENGTH, INNER), 1.0, 6.0, ((1, 4), (2, 4)))
    step_raw = jnp.clip(-3.0 + 4.0 * jax.random.uniform(own_keys[2], (LENGTH, INNER), jnp.float32) ** levels(own_keys[2], (LENGTH, INNER), ((0, 4), (1, 4)), -0.2, 0.2), -3.0, 1.0).astype(jnp.bfloat16)
    state_maps = bell_draw(own_keys[3], (2, NSTATE, LENGTH), 0.3, 2.0, ((2, 4),))
    decay_rate = jnp.clip(jnp.exp(math.log(0.04) - 6.015181 * jax.random.uniform(seeds[4], (NSTATE, INNER), jnp.float32) ** levels(seeds[4], (NSTATE, INNER), ((1, 4),), -0.2, 0.2)), 9.765625145519152e-05, 0.04)
    skip_gain = jnp.clip(0.5 + 1.0 * jax.random.uniform(seeds[5], (INNER,), jnp.float32) ** levels(seeds[5], (INNER,), ((0, 4),), -0.2, 0.2), 0.5, 1.5)
    out_weight = bell_draw(seeds[6], (INNER, D), INNER ** -0.5, 0.09375, ((0, 4), (1, 4)))
    norm_gain = jnp.clip(1.0 + 0.18 * jax.random.normal(seeds[7], (D,), jnp.float32), 0.1, 1.9)
    router_weight = bell_draw(seeds[8], (D, EXPERTS), D ** -0.5, 0.125)
    expert_ids_keys = jax.random.split(jax.random.fold_in(own_keys[9], 1), LENGTH // TOK_DEV)
    expert_ids_turns = jax.random.permutation(jax.random.fold_in(own_keys[9], 3), LENGTH // TOK_DEV)
    expert_ids = jax.vmap(lambda own, number: assign_block(jax.random.fold_in(own_keys[9], 2), own, number, TOK_DEV, EXPERTS, 2, CAP, 2))(expert_ids_keys, expert_ids_turns).reshape((LENGTH, TOPK))
    gate_weight = bell_draw(seeds[10], (EXPERTS, D, FF), D ** -0.5, 0.125, ((0, 4), (2, 4)))
    up_weight = bell_draw(seeds[11], (EXPERTS, D, FF), D ** -0.5, 0.125, ((0, 4), (2, 4)))
    down_weight = bell_draw(seeds[12], (EXPERTS, FF, D), FF ** -0.5, 0.0625, ((0, 4), (1, 4)))
    return {"residual": residual, "mixer_input": mixer_input, "step_raw": step_raw, "state_maps": state_maps, "decay_rate": decay_rate, "skip_gain": skip_gain, "out_weight": out_weight, "norm_gain": norm_gain, "router_weight": router_weight, "expert_ids": expert_ids, "gate_weight": gate_weight, "up_weight": up_weight, "down_weight": down_weight}


def storage_positions():
    rows = jnp.arange(LENGTH, dtype=jnp.int32)
    shard = rows // SEQ_DEV
    within = rows % SEQ_DEV
    opening = shard * HALF + within
    closing = (2 * N_SEQ - 1 - shard) * HALF + (within - HALF)
    return jnp.where(within < HALF, opening, closing).astype(jnp.int32)

def reference(residual, mixer_input, step_raw, state_maps, decay_rate, skip_gain, out_weight, norm_gain, router_weight, expert_ids, gate_weight, up_weight, down_weight):
    positions = storage_positions()
    order = jnp.zeros((LENGTH,), jnp.int32).at[positions].set(jnp.arange(LENGTH, dtype=jnp.int32))
    inner_x = mixer_input[0][order].astype(jnp.float32)
    gate_in = mixer_input[1][order].astype(jnp.float32)
    step = jax.nn.softplus(step_raw[order].astype(jnp.float32))
    in_map = state_maps[0][:, order].astype(jnp.float32).T
    read_map = state_maps[1][:, order].astype(jnp.float32).T

    def advance(state, inputs):
        step_now, map_in, map_read, x_now = inputs
        state = jnp.exp(-step_now[None, :] * decay_rate) * state + (step_now * x_now)[None, :] * map_in[:, None]
        return (state, lax.optimization_barrier(jnp.sum(map_read[:, None] * state, axis=0)))
    start_state = jnp.zeros((NSTATE, INNER), jnp.float32)
    _, readout = lax.scan(advance, start_state, (step, in_map, read_map, inner_x))
    mixed = ((readout + skip_gain[None, :] * inner_x) * jax.nn.silu(gate_in)).astype(jnp.bfloat16)
    mixed = mixed[positions]
    stream = (residual.astype(jnp.float32) + jnp.dot(mixed, out_weight, preferred_element_type=jnp.float32)).astype(jnp.bfloat16)
    stream_f = stream.astype(jnp.float32)
    mean_sq = lax.optimization_barrier(jnp.mean(stream_f * stream_f, axis=-1, keepdims=True))
    normed = (stream_f * lax.rsqrt(mean_sq + 1e-05) * norm_gain[None, :]).astype(jnp.bfloat16)
    logits = jnp.dot(normed, router_weight, preferred_element_type=jnp.float32)
    onehot = (expert_ids[:, :, None] == jnp.arange(EXPERTS, dtype=jnp.int32)[None, None, :]).astype(jnp.float32)
    chosen = lax.optimization_barrier(jnp.sum(onehot * logits[:, None, :], axis=-1))
    weights = jnp.stack([jax.nn.sigmoid(chosen[:, 0] - chosen[:, 1]), jax.nn.sigmoid(chosen[:, 1] - chosen[:, 0])], axis=1)
    ndev = LENGTH // TOK_DEV
    ids_dev = expert_ids.reshape(ndev, TOK_DEV * TOPK)
    hot = (ids_dev[:, :, None] == jnp.arange(EXPERTS, dtype=jnp.int32)[None, None, :]).astype(jnp.int32)
    slot = lax.optimization_barrier(jnp.sum((jnp.cumsum(hot, axis=1) - hot) * hot, axis=-1)).astype(jnp.int32)
    dev_index = jnp.broadcast_to(jnp.arange(ndev, dtype=jnp.int32)[:, None], ids_dev.shape)
    normed_rep = jnp.repeat(normed, TOPK, axis=0).reshape(ndev, TOK_DEV * TOPK, D)
    buffers = jnp.zeros((EXPERTS, ndev, CAP, D), jnp.bfloat16).at[ids_dev, dev_index, slot].set(normed_rep)
    buffers = buffers.reshape(EXPERTS, ndev * CAP, D)
    block = FF // N_SEQ

    def expert(inputs):
        rows, w_gate, w_up, w_down = inputs
        gate = jnp.dot(rows, w_gate, preferred_element_type=jnp.float32)
        upper = jnp.dot(rows, w_up, preferred_element_type=jnp.float32)
        hidden = (jax.nn.silu(gate) * upper).astype(jnp.bfloat16)

        def add_block(total, index):
            begin = (index * block).astype(jnp.int32)
            part_h = lax.dynamic_slice_in_dim(hidden, begin, block, 1)
            part_w = lax.dynamic_slice_in_dim(w_down, begin, block, 0)
            partial_value = jnp.dot(part_h, part_w, preferred_element_type=jnp.float32).astype(jnp.bfloat16)
            partial_value = lax.optimization_barrier(partial_value)
            return (total + partial_value.astype(jnp.float32), None)
        total, _ = lax.scan(add_block, jnp.zeros((ndev * CAP, D), jnp.float32), jnp.arange(N_SEQ, dtype=jnp.int32))
        return total.astype(jnp.bfloat16)
    outputs = lax.map(expert, (buffers, gate_weight, up_weight, down_weight))
    outputs = outputs.reshape(EXPERTS, ndev, CAP, D)
    picked = outputs[ids_dev, dev_index, slot].reshape(LENGTH, TOPK, D).astype(jnp.float32)
    result = stream_f + lax.optimization_barrier(jnp.sum(weights[:, :, None] * picked, axis=1))
    return result.astype(jnp.bfloat16)
```

```python
import functools

import jax
import jax.numpy as jnp
from jax import lax
from jax.experimental import pallas as pl
from jax.experimental.pallas import tpu as pltpu
from jax.sharding import PartitionSpec as P

LOG2E = 1.4426950408889634
f32 = jnp.float32
bf16 = jnp.bfloat16
VMEM = pl.BlockSpec(memory_space=pltpu.VMEM)
SMEM = pl.BlockSpec(memory_space=pltpu.SMEM)


def softplus(v):
    return jnp.maximum(v, 0.0) + jnp.log1p(jnp.exp(-jnp.abs(v)))


def ends_kernel(maps_ref, raw_ref, mixer_ref, dec_ref, pack_ref, step_ref, drive_ref):
    rows, channels = raw_ref.shape
    groups = channels // 128
    states = dec_ref.shape[0]
    half = rows // 2

    @pl.loop(0, rows // 16)
    def _(t):
        for g in range(groups):
            lanes = slice(g * 128, (g + 1) * 128)
            at = pl.ds(t * 16, 16)
            step = softplus(raw_ref[at, lanes].astype(f32))
            to = pl.ds(t * 16 * groups + g, 16, stride=groups)
            step_ref[to, :] = step
            drive_ref[to, :] = step * mixer_ref[0, at, lanes].astype(f32)

    def advance(p, carry):
        total, state = list(carry[0]), [list(v) for v in carry[1]]
        for b in range(2):
            pos = b * half + p
            step = step_ref[pl.ds(pos * groups, groups), :]
            drive = drive_ref[pl.ds(pos * groups, groups), :]
            total[b] = total[b] + step
            for n in range(states):
                decay = jnp.exp2(step * dec_ref[n])
                state[b][n] = decay * state[b][n] + drive * maps_ref[n, pos]
        return tuple(total), tuple(tuple(v) for v in state)

    zero = jnp.zeros((groups, 128), f32)
    total, state = lax.fori_loop(
        0, half, advance, ((zero,) * 2, ((zero,) * states,) * 2), unroll=4
    )
    per = 16 // groups
    for b in range(2):
        for n in range(0, states, per):
            values = jnp.concatenate(state[b][n : n + per], axis=0)
            pack_ref[b, pl.ds(n * groups, 16), :] = values.astype(bf16)
        high = total[b].astype(bf16)
        low = (total[b] - high.astype(f32)).astype(bf16)
        pack_ref[b, pl.ds(states * groups, groups), :] = high
        pack_ref[b, pl.ds((states + 1) * groups, groups), :] = low


def scan_kernel(count, place_ref, maps_ref, step_ref, drive_ref, dec_ref, mixer_ref, skip_ref, *rest):
    packs, (out_ref, all_ref, y_ref) = rest[:count], rest[count:]
    rows, channels = out_ref.shape
    groups = channels // 128
    states = dec_ref.shape[0]
    half = rows // 2
    place = place_ref[0]
    for k in range(count):
        all_ref[k] = packs[k][...].astype(f32)

    def fold(b, carry):
        running, first, second = carry
        opening = b < count
        owner = jnp.where(opening, b, 2 * count - 1 - b)
        slot = lax.rem(place - owner + count, count)
        side = jnp.where(opening, 0, 1)
        total = (
            all_ref[slot, side, pl.ds(states * groups, groups), :]
            + all_ref[slot, side, pl.ds((states + 1) * groups, groups), :]
        )
        first = [jnp.where(b == place, r, f) for r, f in zip(running, first)]
        second = [jnp.where(b == 2 * count - 1 - place, r, s) for r, s in zip(running, second)]
        running = [
            jnp.exp2(total * dec_ref[n]) * running[n]
            + all_ref[slot, side, pl.ds(n * groups, groups), :]
            for n in range(states)
        ]
        return running, first, second

    zeros = [all_ref[0, 0, pl.ds(0, groups), :] * 0.0] * states
    _, first, second = lax.fori_loop(0, 2 * count, fold, (zeros, zeros, zeros))

    def advance(p, state):
        state = [list(v) for v in state]
        for b in range(2):
            pos = b * half + p
            at = pl.ds(pos * groups, groups)
            step = step_ref[at, :]
            drive = drive_ref[at, :]
            parts = [None, None]
            for n in range(states):
                decay = jnp.exp2(step * dec_ref[n])
                state[b][n] = decay * state[b][n] + drive * maps_ref[n, pos]
                term = state[b][n] * maps_ref[states + n, pos]
                parts[n % 2] = term if parts[n % 2] is None else parts[n % 2] + term
            y_ref[at, :] = parts[0] + parts[1]
        return tuple(tuple(v) for v in state)

    lax.fori_loop(0, half, advance, (tuple(first), tuple(second)), unroll=4)

    @pl.loop(0, rows // 16)
    def _(t):
        for g in range(groups):
            lanes = slice(g * 128, (g + 1) * 128)
            at = pl.ds(t * 16, 16)
            y = y_ref[pl.ds(t * 16 * groups + g, 16, stride=groups), :]
            x = mixer_ref[0, at, lanes].astype(f32)
            z = mixer_ref[1, at, lanes].astype(f32)
            out_ref[at, lanes] = ((y + skip_ref[:, lanes] * x) * (z * jax.nn.sigmoid(z))).astype(bf16)


def shift(count, k):
    return [(i, (i + k) % count) for i in range(count)]


def mix(mixer_input, step_raw, state_maps, decay_rate, skip_gain):
    rows, channels = step_raw.shape
    groups = channels // 128
    states = decay_rate.shape[0]
    seq_count = lax.axis_size("seq")
    maps = state_maps.reshape(2 * states, rows).astype(f32)
    dec = (-LOG2E * decay_rate).reshape(states, groups, 128)
    shape = jax.ShapeDtypeStruct
    pack, step, drive = pl.pallas_call(
        ends_kernel,
        out_shape=(
            shape((2, (states + 2) * groups, 128), bf16),
            shape((rows * groups, 128), f32),
            shape((rows * groups, 128), f32),
        ),
        in_specs=[SMEM] + [VMEM] * 3,
        out_specs=(VMEM,) * 3,
        compiler_params=pltpu.CompilerParams(vmem_limit_bytes=24 << 20),
        name="ends",
    )(maps, step_raw, mixer_input, dec)
    packs = [pack] + [lax.ppermute(pack, "seq", shift(seq_count, k)) for k in range(1, seq_count)]
    place = lax.axis_index("seq").astype(jnp.int32).reshape(1)
    return pl.pallas_call(
        functools.partial(scan_kernel, seq_count),
        out_shape=shape((rows, channels), bf16),
        in_specs=[SMEM] * 2 + [VMEM] * (5 + seq_count),
        out_specs=VMEM,
        scratch_shapes=[
            pltpu.VMEM((seq_count, 2, (states + 2) * groups, 128), f32),
            pltpu.VMEM((rows * groups, 128), f32),
        ],
        compiler_params=pltpu.CompilerParams(vmem_limit_bytes=32 << 20),
        name="scan",
    )(place, maps, step, drive, dec, mixer_input, skip_gain[None, :], *packs)


def fetch_weight(out_weight):
    seq_count = lax.axis_size("seq")
    rows = out_weight.shape[0] // 2
    group = lax.axis_index("groups")
    mine = lax.dynamic_slice_in_dim(out_weight, group * rows, rows, 0)
    blocks = []
    for k in range(1, seq_count):
        direct = lax.ppermute(mine, "seq", shift(seq_count, k))
        other = lax.ppermute(direct, "groups", [(0, 1), (1, 0)])
        blocks.append((direct, other))
    return blocks


def project(mixed, out_weight, blocks):
    seq_count = lax.axis_size("seq")
    rows = out_weight.shape[0] // 2
    group = lax.axis_index("groups")
    near = lax.dynamic_slice_in_dim(mixed, group * rows, rows, 1)
    far = lax.dynamic_slice_in_dim(mixed, (1 - group) * rows, rows, 1)
    parts = [jnp.dot(mixed, out_weight, preferred_element_type=f32)]
    for direct, other in blocks:
        parts.append(
            jnp.dot(near, direct, preferred_element_type=f32)
            + jnp.dot(far, other, preferred_element_type=f32)
        )
    return parts


def own_order(parts, axis):
    count = len(parts)
    width = parts[0].shape[axis]
    ring = jnp.concatenate(parts[::-1] * 2, axis=axis)
    start = lax.rem(2 * count - 1 - lax.axis_index("seq"), count) * width
    return lax.dynamic_slice_in_dim(ring, start, count * width, axis)


def sum_to_owner(values):
    exp_count = lax.axis_size("exp")
    chips = exp_count // 2
    place = lax.axis_index("exp")
    chip, core = place // 2, place % 2
    rows = values.shape[0] // exp_count
    shaped = values.reshape(chips, 2, rows, values.shape[1])
    away = lax.dynamic_index_in_dim(shaped, 1 - core, 1, False)
    keep = lax.dynamic_index_in_dim(shaped, core, 1, False)
    pair = keep + lax.ppermute(away, "exp", [(i, i ^ 1) for i in range(exp_count)])
    total = lax.dynamic_index_in_dim(pair, chip, 0, False)
    for j in range(1, chips):
        leaving = lax.dynamic_index_in_dim(pair, (chip + j) % chips, 0, False).astype(bf16)
        total = total + lax.ppermute(leaving, "exp", shift(exp_count, 2 * j)).astype(f32)
    return total


def per_device(
    residual,
    mixer_input,
    step_raw,
    state_maps,
    decay_rate,
    skip_gain,
    out_weight,
    norm_gain,
    router_weight,
    expert_ids,
    gate_weight,
    up_weight,
    down_weight,
):
    blocks = fetch_weight(out_weight)
    mixed = mix(mixer_input, step_raw, state_maps, decay_rate, skip_gain)
    projected = own_order(project(mixed, out_weight, blocks), 1)
    summed = sum_to_owner(projected)
    stream_f = (residual.astype(jnp.float32) + summed).astype(jnp.bfloat16).astype(jnp.float32)
    mean_sq = jnp.mean(stream_f * stream_f, axis=-1, keepdims=True)
    normed = (stream_f * lax.rsqrt(mean_sq + 1e-05) * norm_gain[None, :]).astype(jnp.bfloat16)
    tok_rows = residual.shape[0]
    width = residual.shape[1]
    experts = router_weight.shape[1]
    picks = expert_ids.shape[1]
    capacity = max(2, 8 * tok_rows // (3 * experts))
    logits = jnp.dot(normed, router_weight, preferred_element_type=jnp.float32)
    onehot = (expert_ids[:, :, None] == jnp.arange(experts, dtype=jnp.int32)[None, None, :]).astype(
        jnp.float32
    )
    chosen = jnp.sum(onehot * logits[:, None, :], axis=-1)
    weights = jnp.stack(
        [jax.nn.sigmoid(chosen[:, 0] - chosen[:, 1]), jax.nn.sigmoid(chosen[:, 1] - chosen[:, 0])],
        axis=1,
    )
    flat_ids = expert_ids.reshape(-1)
    hot = (flat_ids[:, None] == jnp.arange(experts, dtype=jnp.int32)[None, :]).astype(jnp.int32)
    slot = jnp.sum((jnp.cumsum(hot, axis=0) - hot) * hot, axis=-1)
    target = flat_ids * capacity + slot
    select = (target[None, :] == jnp.arange(experts * capacity, dtype=jnp.int32)[:, None]).astype(
        jnp.bfloat16
    )
    normed_rep = jnp.repeat(normed, picks, axis=0)
    outgoing = jnp.dot(select, normed_rep, preferred_element_type=jnp.float32).astype(jnp.bfloat16)
    outgoing = outgoing.reshape(experts, capacity, width)
    gate_local = gate_weight[0]
    up_local = up_weight[0]
    down_local = down_weight[0]
    seq_count = lax.axis_size("seq")
    copies = jnp.broadcast_to(outgoing[None], (seq_count,) + outgoing.shape).reshape(
        (seq_count * experts,) + outgoing.shape[1:]
    )
    arrived = lax.all_to_all(copies, ("seq", "exp"), split_axis=0, concat_axis=0, tiled=True)
    flat = arrived.reshape(-1, arrived.shape[-1])
    gate = jnp.dot(flat, gate_local, preferred_element_type=jnp.float32)
    upper = jnp.dot(flat, up_local, preferred_element_type=jnp.float32)
    hidden = (jax.nn.silu(gate) * upper).astype(jnp.bfloat16)
    partial_value = (
        jnp.dot(hidden, down_local, preferred_element_type=jnp.float32)
        .reshape(arrived.shape)
        .astype(jnp.bfloat16)
    )
    back = lax.all_to_all(partial_value, ("seq", "exp"), split_axis=0, concat_axis=0, tiled=True)
    returned = jnp.sum(
        back.astype(jnp.float32).reshape((seq_count, experts) + outgoing.shape[1:]), axis=0
    ).astype(jnp.bfloat16)
    gathered = jnp.dot(
        select.T, returned.reshape(experts * capacity, width), preferred_element_type=jnp.float32
    )
    gathered = gathered.reshape(tok_rows, picks, width)
    result = stream_f + jnp.sum(weights[:, :, None] * gathered, axis=1)
    return result.astype(jnp.bfloat16)


def solution(mesh):
    in_specs = (
        P(("groups", "seq", "exp"), None),
        P(None, ("groups", "seq"), "exp"),
        P(("groups", "seq"), "exp"),
        P(None, None, ("groups", "seq")),
        P(None, "exp"),
        P("exp"),
        P("exp", "seq"),
        P(),
        P(),
        P(("groups", "seq", "exp"), None),
        P("exp", None, "seq"),
        P("exp", None, "seq"),
        P("exp", "seq", None),
    )
    out_specs = P(("groups", "seq", "exp"), None)
    return jax.shard_map(
        per_device, mesh=mesh, in_specs=in_specs, out_specs=out_specs, check_vma=False
    )
```

```python
import functools

import jax
import jax.numpy as jnp
from jax import lax
from jax.experimental import pallas as pl
from jax.experimental.pallas import tpu as pltpu
from jax.sharding import PartitionSpec as P

LOG2E = 1.4426950408889634
f32 = jnp.float32
bf16 = jnp.bfloat16
VMEM = pl.BlockSpec(memory_space=pltpu.VMEM)
SMEM = pl.BlockSpec(memory_space=pltpu.SMEM)


def softplus(v):
    return jnp.maximum(v, 0.0) + jnp.log1p(jnp.exp(-jnp.abs(v)))


def ends_kernel(maps_ref, raw_ref, mixer_ref, dec_ref, pack_ref, step_ref, drive_ref):
    rows, channels = raw_ref.shape
    groups = channels // 128
    states = dec_ref.shape[0]
    half = rows // 2

    @pl.loop(0, rows // 16)
    def _(t):
        for g in range(groups):
            lanes = slice(g * 128, (g + 1) * 128)
            at = pl.ds(t * 16, 16)
            step = softplus(raw_ref[at, lanes].astype(f32))
            to = pl.ds(t * 16 * groups + g, 16, stride=groups)
            step_ref[to, :] = step
            drive_ref[to, :] = step * mixer_ref[0, at, lanes].astype(f32)

    def advance(p, carry):
        total, state = list(carry[0]), [list(v) for v in carry[1]]
        for b in range(2):
            pos = b * half + p
            step = step_ref[pl.ds(pos * groups, groups), :]
            drive = drive_ref[pl.ds(pos * groups, groups), :]
            total[b] = total[b] + step
            for n in range(states):
                decay = jnp.exp2(step * dec_ref[n])
                state[b][n] = decay * state[b][n] + drive * maps_ref[n, pos]
        return tuple(total), tuple(tuple(v) for v in state)

    zero = jnp.zeros((groups, 128), f32)
    total, state = lax.fori_loop(
        0, half, advance, ((zero,) * 2, ((zero,) * states,) * 2), unroll=4
    )
    per = 16 // groups
    for b in range(2):
        for n in range(0, states, per):
            values = jnp.concatenate(state[b][n : n + per], axis=0)
            pack_ref[b, pl.ds(n * groups, 16), :] = values.astype(bf16)
        high = total[b].astype(bf16)
        low = (total[b] - high.astype(f32)).astype(bf16)
        pack_ref[b, pl.ds(states * groups, groups), :] = high
        pack_ref[b, pl.ds((states + 1) * groups, groups), :] = low


def scan_kernel(count, place_ref, maps_ref, step_ref, drive_ref, dec_ref, mixer_ref, skip_ref, *rest):
    packs, (out_ref, all_ref, y_ref) = rest[:count], rest[count:]
    rows, channels = out_ref.shape
    groups = channels // 128
    states = dec_ref.shape[0]
    half = rows // 2
    place = place_ref[0]
    for k in range(count):
        all_ref[k] = packs[k][...].astype(f32)

    def fold(b, carry):
        running, first, second = carry
        opening = b < count
        owner = jnp.where(opening, b, 2 * count - 1 - b)
        slot = lax.rem(place - owner + count, count)
        side = jnp.where(opening, 0, 1)
        total = (
            all_ref[slot, side, pl.ds(states * groups, groups), :]
            + all_ref[slot, side, pl.ds((states + 1) * groups, groups), :]
        )
        first = [jnp.where(b == place, r, f) for r, f in zip(running, first)]
        second = [jnp.where(b == 2 * count - 1 - place, r, s) for r, s in zip(running, second)]
        running = [
            jnp.exp2(total * dec_ref[n]) * running[n]
            + all_ref[slot, side, pl.ds(n * groups, groups), :]
            for n in range(states)
        ]
        return running, first, second

    zeros = [all_ref[0, 0, pl.ds(0, groups), :] * 0.0] * states
    _, first, second = lax.fori_loop(0, 2 * count, fold, (zeros, zeros, zeros))

    def advance(p, state):
        state = [list(v) for v in state]
        for b in range(2):
            pos = b * half + p
            at = pl.ds(pos * groups, groups)
            step = step_ref[at, :]
            drive = drive_ref[at, :]
            parts = [None, None]
            for n in range(states):
                decay = jnp.exp2(step * dec_ref[n])
                state[b][n] = decay * state[b][n] + drive * maps_ref[n, pos]
                term = state[b][n] * maps_ref[states + n, pos]
                parts[n % 2] = term if parts[n % 2] is None else parts[n % 2] + term
            y_ref[at, :] = parts[0] + parts[1]
        return tuple(tuple(v) for v in state)

    lax.fori_loop(0, half, advance, (tuple(first), tuple(second)), unroll=4)

    @pl.loop(0, rows // 16)
    def _(t):
        for g in range(groups):
            lanes = slice(g * 128, (g + 1) * 128)
            at = pl.ds(t * 16, 16)
            y = y_ref[pl.ds(t * 16 * groups + g, 16, stride=groups), :]
            x = mixer_ref[0, at, lanes].astype(f32)
            z = mixer_ref[1, at, lanes].astype(f32)
            out_ref[at, lanes] = ((y + skip_ref[:, lanes] * x) * (z * jax.nn.sigmoid(z))).astype(bf16)


def shift(count, k):
    return [(i, (i + k) % count) for i in range(count)]


def mix(mixer_input, step_raw, state_maps, decay_rate, skip_gain):
    rows, channels = step_raw.shape
    groups = channels // 128
    states = decay_rate.shape[0]
    seq_count = lax.axis_size("seq")
    maps = state_maps.reshape(2 * states, rows).astype(f32)
    dec = (-LOG2E * decay_rate).reshape(states, groups, 128)
    shape = jax.ShapeDtypeStruct
    pack, step, drive = pl.pallas_call(
        ends_kernel,
        out_shape=(
            shape((2, (states + 2) * groups, 128), bf16),
            shape((rows * groups, 128), f32),
            shape((rows * groups, 128), f32),
        ),
        in_specs=[SMEM] + [VMEM] * 3,
        out_specs=(VMEM,) * 3,
        compiler_params=pltpu.CompilerParams(vmem_limit_bytes=24 << 20),
        name="ends",
    )(maps, step_raw, mixer_input, dec)
    packs = [pack] + [lax.ppermute(pack, "seq", shift(seq_count, k)) for k in range(1, seq_count)]
    place = lax.axis_index("seq").astype(jnp.int32).reshape(1)
    return pl.pallas_call(
        functools.partial(scan_kernel, seq_count),
        out_shape=shape((rows, channels), bf16),
        in_specs=[SMEM] * 2 + [VMEM] * (5 + seq_count),
        out_specs=VMEM,
        scratch_shapes=[
            pltpu.VMEM((seq_count, 2, (states + 2) * groups, 128), f32),
            pltpu.VMEM((rows * groups, 128), f32),
        ],
        compiler_params=pltpu.CompilerParams(vmem_limit_bytes=32 << 20),
        name="scan",
    )(place, maps, step, drive, dec, mixer_input, skip_gain[None, :], *packs)


def fetch_weight(out_weight):
    seq_count = lax.axis_size("seq")
    rows = out_weight.shape[0] // 2
    group = lax.axis_index("groups")
    mine = lax.dynamic_slice_in_dim(out_weight, group * rows, rows, 0)
    blocks = []
    for k in range(1, seq_count):
        direct = lax.ppermute(mine, "seq", shift(seq_count, k))
        other = lax.ppermute(direct, "groups", [(0, 1), (1, 0)])
        blocks.append((direct, other))
    return blocks


def project(mixed, out_weight, blocks):
    seq_count = lax.axis_size("seq")
    rows = out_weight.shape[0] // 2
    group = lax.axis_index("groups")
    near = lax.dynamic_slice_in_dim(mixed, group * rows, rows, 1)
    far = lax.dynamic_slice_in_dim(mixed, (1 - group) * rows, rows, 1)
    parts = [jnp.dot(mixed, out_weight, preferred_element_type=f32)]
    for direct, other in blocks:
        parts.append(
            jnp.dot(near, direct, preferred_element_type=f32)
            + jnp.dot(far, other, preferred_element_type=f32)
        )
    return parts


def own_order(parts, axis):
    count = len(parts)
    width = parts[0].shape[axis]
    ring = jnp.concatenate(parts[::-1] * 2, axis=axis)
    start = lax.rem(2 * count - 1 - lax.axis_index("seq"), count) * width
    return lax.dynamic_slice_in_dim(ring, start, count * width, axis)


def sum_to_owner(values):
    exp_count = lax.axis_size("exp")
    chips = exp_count // 2
    place = lax.axis_index("exp")
    chip, core = place // 2, place % 2
    rows = values.shape[0] // exp_count
    shaped = values.reshape(chips, 2, rows, values.shape[1])
    away = lax.dynamic_index_in_dim(shaped, 1 - core, 1, False)
    keep = lax.dynamic_index_in_dim(shaped, core, 1, False)
    pair = keep + lax.ppermute(away, "exp", [(i, i ^ 1) for i in range(exp_count)])
    total = lax.dynamic_index_in_dim(pair, chip, 0, False)
    for j in range(1, chips):
        leaving = lax.dynamic_index_in_dim(pair, (chip + j) % chips, 0, False).astype(bf16)
        total = total + lax.ppermute(leaving, "exp", shift(exp_count, 2 * j)).astype(f32)
    return total


def pack_tokens(normed, router_weight, expert_ids):
    rows = normed.shape[0]
    experts = router_weight.shape[1]
    logits = jnp.dot(normed, router_weight, preferred_element_type=f32)
    lane = jnp.arange(experts, dtype=jnp.int32)[None, :]
    first = expert_ids[:, 0:1] == lane
    second = expert_ids[:, 1:2] == lane
    gap = jnp.sum(jnp.where(first, logits, 0.0) - jnp.where(second, logits, 0.0), axis=1, keepdims=True)
    weight = jnp.where(first, jax.nn.sigmoid(gap), 0.0) + jnp.where(second, jax.nn.sigmoid(-gap), 0.0)
    routed = first | second
    earlier = jnp.arange(rows)[:, None] > jnp.arange(rows)[None, :]
    slot = jnp.dot(earlier.astype(bf16), routed.astype(bf16), preferred_element_type=f32)
    high = weight.astype(bf16)
    low = (weight - high.astype(f32)).astype(bf16)
    slot = jnp.where(routed, slot + 1.0, 0.0).astype(bf16)
    blank = jnp.zeros((rows, 128 - 3 * experts), bf16)
    return jnp.concatenate([normed, high, low, slot, blank], axis=1)


def expert_part(tokens, capacity, block_rows, experts, gate, up, down):
    width = tokens.shape[1] - 128
    count = tokens.shape[0] // block_rows
    place = lax.axis_index("exp")
    lane = jnp.arange(128, dtype=jnp.int32)[None, :]
    slot = jnp.sum(jnp.where(lane == 2 * experts + place, tokens[:, width:].astype(f32), 0.0), axis=1)
    block = jnp.arange(tokens.shape[0], dtype=jnp.int32) // block_rows
    target = jnp.where(slot > 0.0, block * capacity + slot.astype(jnp.int32) - 1, -1)
    chosen = (target[None, :] == jnp.arange(count * capacity, dtype=jnp.int32)[:, None]).astype(bf16)
    held = jnp.dot(chosen, tokens, preferred_element_type=f32).astype(bf16)
    mine = (lane == place) | (lane == experts + place)
    weight = jnp.sum(jnp.where(mine, held[:, width:].astype(f32), 0.0), axis=1, keepdims=True)
    rows = held[:, :width]
    gated = jnp.dot(rows, gate, preferred_element_type=f32)
    upper = jnp.dot(rows, up, preferred_element_type=f32)
    hidden = (jax.nn.silu(gated) * upper).astype(bf16)
    partial_value = jnp.dot(hidden, down, preferred_element_type=f32)
    scaled = (partial_value * weight).astype(bf16)
    return lax.dot_general(chosen, scaled, (((0,), (0,)), ((), ())), preferred_element_type=f32)


def experts_sum(packed, experts, capacity, gate, up, down):
    seq_count = lax.axis_size("seq")
    exp_count = lax.axis_size("exp")
    chips = exp_count // 2
    rows = packed.shape[0]
    width = packed.shape[1] - 128
    partner = [(i, i ^ 1) for i in range(exp_count)]
    order = [k for pair in zip(range(1, seq_count), range(seq_count - 1, 0, -1)) for k in pair]
    order = list(dict.fromkeys(order))

    planes = {0: packed}
    for k in order:
        planes[k] = lax.ppermute(packed, "seq", shift(seq_count, k))

    total = None
    for k in order[:-1] + [0] + order[-1:]:
        row = [planes[k]]
        for j in range(1, chips):
            row.append(lax.ppermute(planes[k], "exp", shift(exp_count, 2 * j)))
        row = jnp.concatenate(row, axis=0)
        both = jnp.concatenate([row, lax.ppermute(row, "exp", partner)], axis=0)
        part = expert_part(both, capacity, rows, experts, gate, up, down)
        held = chips * rows
        pair = part[:held] + lax.ppermute(part[held:].astype(bf16), "exp", partner).astype(f32)
        mine = pair[:rows]
        for j in range(1, chips):
            leaving = pair[j * rows : (j + 1) * rows].astype(bf16)
            mine = mine + lax.ppermute(leaving, "exp", shift(exp_count, exp_count - 2 * j)).astype(f32)
        if k:
            mine = lax.ppermute(mine.astype(bf16), "seq", shift(seq_count, seq_count - k)).astype(f32)
        total = mine if total is None else total + mine
    return total


def per_device(
    residual,
    mixer_input,
    step_raw,
    state_maps,
    decay_rate,
    skip_gain,
    out_weight,
    norm_gain,
    router_weight,
    expert_ids,
    gate_weight,
    up_weight,
    down_weight,
):
    blocks = fetch_weight(out_weight)
    mixed = mix(mixer_input, step_raw, state_maps, decay_rate, skip_gain)
    projected = own_order(project(mixed, out_weight, blocks), 1)
    summed = sum_to_owner(projected)
    stream_f = (residual.astype(jnp.float32) + summed).astype(jnp.bfloat16).astype(jnp.float32)
    mean_sq = jnp.mean(stream_f * stream_f, axis=-1, keepdims=True)
    normed = (stream_f * lax.rsqrt(mean_sq + 1e-05) * norm_gain[None, :]).astype(jnp.bfloat16)
    tok_rows = residual.shape[0]
    experts = router_weight.shape[1]
    capacity = max(2, 8 * tok_rows // (3 * experts))
    packed = pack_tokens(normed, router_weight, expert_ids)
    added = experts_sum(packed, experts, capacity, gate_weight[0], up_weight[0], down_weight[0])
    return (stream_f + added).astype(jnp.bfloat16)


def solution(mesh):
    in_specs = (
        P(("groups", "seq", "exp"), None),
        P(None, ("groups", "seq"), "exp"),
        P(("groups", "seq"), "exp"),
        P(None, None, ("groups", "seq")),
        P(None, "exp"),
        P("exp"),
        P("exp", "seq"),
        P(),
        P(),
        P(("groups", "seq", "exp"), None),
        P("exp", None, "seq"),
        P("exp", None, "seq"),
        P("exp", "seq", None),
    )
    out_specs = P(("groups", "seq", "exp"), None)
    return jax.shard_map(
        per_device, mesh=mesh, in_specs=in_specs, out_specs=out_specs, check_vma=False
    )
```

```python
import functools

import jax
import jax.numpy as jnp
from jax import lax
from jax.experimental import pallas as pl
from jax.experimental.pallas import tpu as pltpu
from jax.sharding import PartitionSpec as P

LOG2E = 1.4426950408889634
f32 = jnp.float32
bf16 = jnp.bfloat16
VMEM_EXPERT = 16
VMEM = pl.BlockSpec(memory_space=pltpu.VMEM)
SMEM = pl.BlockSpec(memory_space=pltpu.SMEM)


def softplus(v):
    return jnp.maximum(v, 0.0) + jnp.log1p(jnp.exp(-jnp.abs(v)))


def load_decay(rate_ref, dec_ref):
    states, groups = dec_ref.shape[0] * 128 // rate_ref.shape[1], rate_ref.shape[1] // 128
    for g in range(groups):
        lanes = slice(g * 128, (g + 1) * 128)
        dec_ref[pl.ds(g, states, stride=groups), :] = -LOG2E * rate_ref[:, lanes]


def ends_kernel(maps_ref, raw_ref, mixer_ref, rate_ref, pack_ref, step_ref, drive_ref, dec_ref):
    rows, channels = raw_ref.shape
    groups = channels // 128
    states = rate_ref.shape[0]
    half = rows // 2
    load_decay(rate_ref, dec_ref)
    dec = [dec_ref[pl.ds(n * groups, groups), :] for n in range(states)]

    @pl.loop(0, rows // 16)
    def _(t):
        for g in range(groups):
            lanes = slice(g * 128, (g + 1) * 128)
            at = pl.ds(t * 16, 16)
            step = softplus(raw_ref[at, lanes].astype(f32))
            to = pl.ds(t * 16 * groups + g, 16, stride=groups)
            step_ref[to, :] = step
            drive_ref[to, :] = step * mixer_ref[0, at, lanes].astype(f32)

    def advance(p, carry):
        total, state = list(carry[0]), [list(v) for v in carry[1]]
        for b in range(2):
            pos = b * half + p
            step = step_ref[pl.ds(pos * groups, groups), :]
            drive = drive_ref[pl.ds(pos * groups, groups), :]
            total[b] = total[b] + step
            for n in range(states):
                decay = jnp.exp2(step * dec[n])
                state[b][n] = decay * state[b][n] + drive * maps_ref[n, pos]
        return tuple(total), tuple(tuple(v) for v in state)

    zero = jnp.zeros((groups, 128), f32)
    total, state = lax.fori_loop(
        0, half, advance, ((zero,) * 2, ((zero,) * states,) * 2), unroll=4
    )
    per = 16 // groups
    for b in range(2):
        for n in range(0, states, per):
            values = jnp.concatenate(state[b][n : n + per], axis=0)
            pack_ref[b, pl.ds(n * groups, 16), :] = values.astype(bf16)
        high = total[b].astype(bf16)
        low = (total[b] - high.astype(f32)).astype(bf16)
        pack_ref[b, pl.ds(states * groups, groups), :] = high
        pack_ref[b, pl.ds((states + 1) * groups, groups), :] = low


def scan_kernel(count, maps_ref, step_ref, drive_ref, rate_ref, mixer_ref, skip_ref, *rest):
    packs, (out_ref, all_ref, y_ref, dec_ref) = rest[:count], rest[count:]
    rows, channels = out_ref.shape
    groups = channels // 128
    states = rate_ref.shape[0]
    load_decay(rate_ref, dec_ref)
    dec = [dec_ref[pl.ds(n * groups, groups), :] for n in range(states)]
    half = rows // 2
    place = lax.axis_index("seq")
    for k in range(count):
        all_ref[k] = packs[k][...].astype(f32)

    def fold(b, carry):
        running, first, second = carry
        opening = b < count
        owner = jnp.where(opening, b, 2 * count - 1 - b)
        slot = lax.rem(place - owner + count, count)
        side = jnp.where(opening, 0, 1)
        total = (
            all_ref[slot, side, pl.ds(states * groups, groups), :]
            + all_ref[slot, side, pl.ds((states + 1) * groups, groups), :]
        )
        first = [jnp.where(b == place, r, f) for r, f in zip(running, first)]
        second = [jnp.where(b == 2 * count - 1 - place, r, s) for r, s in zip(running, second)]
        running = [
            jnp.exp2(total * dec[n]) * running[n]
            + all_ref[slot, side, pl.ds(n * groups, groups), :]
            for n in range(states)
        ]
        return running, first, second

    zeros = [all_ref[0, 0, pl.ds(0, groups), :] * 0.0] * states
    _, first, second = lax.fori_loop(0, 2 * count, fold, (zeros, zeros, zeros))

    def advance(p, state):
        state = [list(v) for v in state]
        for b in range(2):
            pos = b * half + p
            at = pl.ds(pos * groups, groups)
            step = step_ref[at, :]
            drive = drive_ref[at, :]
            parts = [None, None]
            for n in range(states):
                decay = jnp.exp2(step * dec[n])
                state[b][n] = decay * state[b][n] + drive * maps_ref[n, pos]
                term = state[b][n] * maps_ref[states + n, pos]
                parts[n % 2] = term if parts[n % 2] is None else parts[n % 2] + term
            y_ref[at, :] = parts[0] + parts[1]
        return tuple(tuple(v) for v in state)

    lax.fori_loop(0, half, advance, (tuple(first), tuple(second)), unroll=4)

    @pl.loop(0, rows // 16)
    def _(t):
        for g in range(groups):
            lanes = slice(g * 128, (g + 1) * 128)
            at = pl.ds(t * 16, 16)
            y = y_ref[pl.ds(t * 16 * groups + g, 16, stride=groups), :]
            x = mixer_ref[0, at, lanes].astype(f32)
            z = mixer_ref[1, at, lanes].astype(f32)
            out_ref[at, lanes] = ((y + skip_ref[:, lanes] * x) * (z * jax.nn.sigmoid(z))).astype(bf16)


def shift(count, k):
    return [(i, (i + k) % count) for i in range(count)]


def after(values, ready):
    return lax.optimization_barrier((values, ready))[0]


def far_order(count):
    order = [k for pair in zip(range(1, count), range(count - 1, 0, -1)) for k in pair]
    return list(dict.fromkeys(order))


def mix(mixer_input, step_raw, state_maps, decay_rate, skip_gain, out_weight):
    rows, channels = step_raw.shape
    groups = channels // 128
    states = decay_rate.shape[0]
    seq_count = lax.axis_size("seq")
    order = far_order(seq_count)
    swap = [(0, 1), (1, 0)]
    half = out_weight.shape[0] // 2
    mine = lax.dynamic_slice_in_dim(out_weight, lax.axis_index("groups") * half, half, 0)
    direct = {order[0]: lax.ppermute(mine, "seq", shift(seq_count, order[0]))}

    maps = state_maps.reshape(2 * states, rows).astype(f32)
    shape = jax.ShapeDtypeStruct
    pack, step, drive = pl.pallas_call(
        ends_kernel,
        out_shape=(
            shape((2, (states + 2) * groups, 128), bf16),
            shape((rows * groups, 128), f32),
            shape((rows * groups, 128), f32),
        ),
        in_specs=[SMEM] + [VMEM] * 3,
        out_specs=(VMEM,) * 3,
        scratch_shapes=[pltpu.VMEM((states * groups, 128), f32)],
        compiler_params=pltpu.CompilerParams(vmem_limit_bytes=8 << 20),
        name="ends",
    )(maps, step_raw, mixer_input, decay_rate)
    packs = {0: pack}
    for k in order:
        packs[k] = lax.ppermute(pack, "seq", shift(seq_count, k))
    packs = [packs[k] for k in range(seq_count)]
    rest = after(mine, packs)
    for k in order[1:]:
        direct[k] = lax.ppermute(rest, "seq", shift(seq_count, k))
    other = {k: lax.ppermute(direct[k], "groups", swap) for k in order}

    mixed = pl.pallas_call(
        functools.partial(scan_kernel, seq_count),
        out_shape=shape((rows, channels), bf16),
        in_specs=[SMEM] + [VMEM] * (5 + seq_count),
        out_specs=VMEM,
        scratch_shapes=[
            pltpu.VMEM((seq_count, 2, (states + 2) * groups, 128), f32),
            pltpu.VMEM((rows * groups, 128), f32),
            pltpu.VMEM((states * groups, 128), f32),
        ],
        compiler_params=pltpu.CompilerParams(vmem_limit_bytes=12 << 20),
        name="scan",
    )(maps, step, drive, decay_rate, mixer_input, skip_gain[None, :], *packs)
    return mixed, [(k, direct[k], other[k]) for k in order]


def project_kernel(kinds, mixed_ref, *refs):
    keep_ref, away_ref = refs[-2:]
    core = lax.rem(lax.axis_index("exp"), 2)
    group = lax.axis_index("groups")
    chips = lax.axis_size("exp") // 2
    rows = mixed_ref.shape[0] // (2 * chips)
    half = mixed_ref.shape[1] // 2
    spans = (
        slice(None),
        pl.ds(pl.multiple_of(group * half, 128), half),
        pl.ds(pl.multiple_of((1 - group) * half, 128), half),
    )
    for to_ref, side in ((keep_ref, core), (away_ref, 1 - core)):
        parts = [
            jnp.concatenate(
                [mixed_ref[pl.ds(pl.multiple_of((2 * x + side) * rows, rows), rows), span] for x in range(chips)],
                axis=0,
            )
            for span in spans
        ]
        at = 0
        used = 0
        for split in kinds:
            width = refs[used].shape[1]
            if split:
                value = jnp.dot(parts[1], refs[used][...], preferred_element_type=f32)
                value += jnp.dot(parts[2], refs[used + 1][...], preferred_element_type=f32)
            else:
                value = jnp.dot(parts[0], refs[used][...], preferred_element_type=f32)
            to_ref[:, at : at + width] = value
            at += width
            used += 2 if split else 1


def project(mixed, pieces):
    kinds = tuple(len(piece) == 2 for piece in pieces)
    arrays = [array for piece in pieces for array in piece]
    width = sum(piece[0].shape[1] for piece in pieces)
    out = jax.ShapeDtypeStruct((mixed.shape[0] // 2, width), f32)
    return pl.pallas_call(
        functools.partial(project_kernel, kinds),
        out_shape=(out, out),
        in_specs=[VMEM] * (1 + len(arrays)),
        out_specs=(VMEM, VMEM),
        compiler_params=pltpu.CompilerParams(vmem_limit_bytes=12 << 20),
        cost_estimate=pl.CostEstimate(
            flops=2 * mixed.size * width, bytes_accessed=2 * mixed.shape[1] * width, transcendentals=0
        ),
        name="project",
    )(mixed, *arrays)


def leave_kernel(keep_ref, theirs_ref, *out_refs):
    chips = len(out_refs) + 1
    chip = lax.axis_index("exp") // 2
    rows = keep_ref.shape[0] // chips
    for j in range(1, chips):
        at = pl.ds(pl.multiple_of(lax.rem(chip + j, chips) * rows, rows), rows)
        out_refs[j - 1][...] = (keep_ref[at, :] + theirs_ref[at, :]).astype(bf16)


def sum_to_owner(keep, away):
    exp_count = lax.axis_size("exp")
    chips = exp_count // 2
    theirs = lax.ppermute(away, "exp", [(i, i ^ 1) for i in range(exp_count)])
    terms = [keep, theirs]
    out = jax.ShapeDtypeStruct((keep.shape[0] // chips, keep.shape[1]), bf16)
    leaving = pl.pallas_call(
        leave_kernel,
        out_shape=(out,) * (chips - 1),
        in_specs=[VMEM] * 2,
        out_specs=(VMEM,) * (chips - 1),
        compiler_params=pltpu.CompilerParams(vmem_limit_bytes=8 << 20),
        name="leave",
    )(keep, theirs)
    for j in range(1, chips):
        terms.append(lax.ppermute(leaving[j - 1], "exp", shift(exp_count, 2 * j)))
    return terms


def route_kernel(sets, experts, *refs):
    count = sum(len(ks) for ks, _ in sets)
    terms_total = sum(terms for _, terms in sets)
    terms, (residual_ref, gain_ref, router_ref, ids_ref) = refs[:terms_total], refs[terms_total : terms_total + 4]
    stream_ref, packed_ref, sum_ref = refs[terms_total + 4 :]
    rows, width = residual_ref.shape
    part = width // count
    place = lax.axis_index("seq")
    mine = pl.ds(pl.multiple_of(lax.axis_index("exp") // 2 * rows, rows), rows)
    used = 0
    for ks, number in sets:
        for i, k in enumerate(ks):
            lanes = slice(i * part, (i + 1) * part)
            value = terms[used][mine, lanes] + terms[used + 1][mine, lanes]
            for extra in range(2, number):
                value = value + terms[used + extra][:, lanes].astype(f32)
            at = pl.multiple_of(lax.rem(place - k + count, count) * part, 128)
            sum_ref[:, pl.ds(at, part)] = value
        used += number
    stream = (residual_ref[...].astype(f32) + sum_ref[...]).astype(bf16)
    stream_ref[...] = stream
    stream = stream.astype(f32)
    mean_sq = jnp.mean(stream * stream, axis=1, keepdims=True)
    normed = (stream * lax.rsqrt(mean_sq + 1e-05) * gain_ref[...]).astype(bf16)
    packed_ref[:, :width] = normed
    logits = jnp.dot(normed, router_ref[...], preferred_element_type=f32)
    row, column = (lax.broadcasted_iota(jnp.int32, (rows, rows), d) for d in range(2))
    same = jnp.where(row == column, 1.0, 0.0).astype(bf16)
    name = lax.broadcasted_iota(jnp.int32, (128, rows), 0)

    def picked(choice):
        hot = jnp.where(ids_ref[choice : choice + 1, :] == name, 1.0, 0.0).astype(bf16)
        return lax.dot_general(same, hot, (((1,), (1,)), ((), ())), preferred_element_type=f32) > 0.5

    first, second = picked(0), picked(1)
    gap = jnp.sum(jnp.where(first, logits, 0.0), axis=1, keepdims=True) - jnp.sum(
        jnp.where(second, logits, 0.0), axis=1, keepdims=True
    )
    weight = jnp.where(first, jax.nn.sigmoid(gap), 0.0) + jnp.where(second, jax.nn.sigmoid(-gap), 0.0)
    routed = jnp.where(first, 1.0, 0.0) + jnp.where(second, 1.0, 0.0)
    earlier = jnp.where(row > column, 1.0, 0.0)
    slot = jnp.dot(earlier.astype(bf16), routed.astype(bf16), preferred_element_type=f32)
    slot = jnp.where(routed > 0.0, slot + 1.0, 0.0)
    high = weight.astype(bf16).astype(f32)
    lanes = high + pltpu.roll(weight - high, experts, 1) + pltpu.roll(slot, 2 * experts, 1)
    packed_ref[:, width:] = lanes.astype(bf16)


def route(sets, residual, norm_gain, router, experts, expert_ids):
    rows, width = residual.shape
    shape = jax.ShapeDtypeStruct
    terms = [term for _, group in sets for term in group]
    kinds = tuple((tuple(ks), len(group)) for ks, group in sets)
    return pl.pallas_call(
        functools.partial(route_kernel, kinds, experts),
        out_shape=(shape((rows, width), bf16), shape((rows, width + 128), bf16)),
        in_specs=[VMEM] * (len(terms) + 4),
        out_specs=(VMEM, VMEM),
        scratch_shapes=[pltpu.VMEM((rows, width), f32)],
        compiler_params=pltpu.CompilerParams(vmem_limit_bytes=8 << 20),
        name="route",
    )(*terms, residual, norm_gain[None, :], router, expert_ids.T)


def expert_kernel(capacity, block_rows, experts, tile, own_ref, mate_ref, gate_ref, up_ref, down_ref, *rest):
    keep_ref, send_ref, acc_ref = rest
    rows, width = keep_ref.shape
    slots = acc_ref.shape[0]
    lane = lax.broadcasted_iota(jnp.int32, (1, 128), 1)
    place = lax.axis_index("exp")
    picked = lane == 2 * experts + place
    wanted = jnp.broadcast_to(jnp.where(picked, 1.0, 0.0), (8, 128)).astype(bf16)
    held = None
    for side, ref in enumerate((own_ref, mate_ref)):
        slot = lax.dot_general(
            wanted, ref[:, width:], (((1,), (1,)), ((), ())), preferred_element_type=f32
        )[0:1, :].astype(jnp.int32)
        block = lax.broadcasted_iota(jnp.int32, (1, rows), 1) // block_rows + side * (rows // block_rows)
        target = jnp.where(slot > 0, block * capacity + slot - 1, -1)
        chosen = jnp.where(lax.broadcasted_iota(jnp.int32, (slots, rows), 0) == target, 1.0, 0.0)
        value = jnp.dot(chosen.astype(bf16), ref[...], preferred_element_type=f32)
        held = value if held is None else held + value
    mine = (lane == place) | (lane == experts + place)
    weight = jnp.sum(jnp.where(mine, held[:, width:], 0.0), axis=1, keepdims=True)
    held = held[:, :width].astype(bf16)

    for t in range(gate_ref.shape[2] // tile):
        at = slice(t * tile, (t + 1) * tile)
        gated = jnp.dot(held, gate_ref[0, :, at], preferred_element_type=f32)
        upper = jnp.dot(held, up_ref[0, :, at], preferred_element_type=f32)
        hidden = (gated * jax.nn.sigmoid(gated) * upper).astype(bf16)
        value = jnp.dot(hidden, down_ref[0, at, :], preferred_element_type=f32)
        if t == 0:
            acc_ref[...] = value
        else:
            acc_ref[...] += value

    scaled = (acc_ref[...] * weight).astype(bf16)
    for side, ref in enumerate((own_ref, mate_ref)):
        slot = jnp.sum(jnp.where(picked, ref[:, width:].astype(f32), 0.0), axis=1, keepdims=True)
        block = lax.broadcasted_iota(jnp.int32, (rows, 1), 0) // block_rows + side * (rows // block_rows)
        target = jnp.where(slot > 0.0, block * capacity + slot.astype(jnp.int32) - 1, -1)
        chosen = jnp.where(lax.broadcasted_iota(jnp.int32, (rows, slots), 1) == target, 1.0, 0.0)
        back = jnp.dot(chosen.astype(bf16), scaled, preferred_element_type=f32)
        if side == 0:
            keep_ref[...] = back
        else:
            send_ref[...] = back.astype(bf16)


def hold_kernel(from_ref, to_ref):
    pltpu.sync_copy(from_ref, to_ref)


def hold(weight, ready):
    return pl.pallas_call(
        hold_kernel,
        out_shape=jax.ShapeDtypeStruct(weight.shape, weight.dtype),
        in_specs=[pl.BlockSpec(memory_space=pl.ANY)],
        out_specs=VMEM,
        compiler_params=pltpu.CompilerParams(vmem_limit_bytes=16 << 20),
        cost_estimate=pl.CostEstimate(flops=0, bytes_accessed=2 * weight.size, transcendentals=0),
        name="hold",
    )(after(weight, ready))


def expert_part(own, mate, capacity, block_rows, experts, gate, up, down):
    rows, width = own.shape[0], own.shape[1] - 128
    hidden = gate.shape[2]
    tile = 256 if hidden % 256 == 0 else hidden
    slots = -(-2 * rows // block_rows * capacity // 16) * 16
    shape = jax.ShapeDtypeStruct
    return pl.pallas_call(
        functools.partial(expert_kernel, capacity, block_rows, experts, tile),
        out_shape=(shape((rows, width), f32), shape((rows, width), bf16)),
        in_specs=[VMEM] * 5,
        out_specs=(VMEM, VMEM),
        scratch_shapes=[pltpu.VMEM((slots, width), f32)],
        compiler_params=pltpu.CompilerParams(vmem_limit_bytes=VMEM_EXPERT << 20),
        cost_estimate=pl.CostEstimate(
            flops=6 * slots * width * hidden,
            bytes_accessed=6 * width * hidden,
            transcendentals=slots * hidden,
        ),
        name="expert",
    )(own, mate, gate, up, down)


def experts_sum(packed, experts, capacity, gate, up, down):
    seq_count = lax.axis_size("seq")
    exp_count = lax.axis_size("exp")
    chips = exp_count // 2
    rows = packed.shape[0]
    partner = [(i, i ^ 1) for i in range(exp_count)]
    order = far_order(seq_count)

    planes = {0: packed}
    for k in order:
        planes[k] = lax.ppermute(packed, "seq", shift(seq_count, k))

    total = None
    for k in [0] + order:
        row = [planes[k]]
        for j in range(1, chips):
            row.append(lax.ppermute(planes[k], "exp", shift(exp_count, 2 * j)))
        row = jnp.concatenate(row, axis=0)
        mate = lax.ppermute(row, "exp", partner)
        keep, send = expert_part(row, mate, capacity, rows, experts, gate, up, down)
        pair = keep + lax.ppermute(send, "exp", partner).astype(f32)
        mine = pair[:rows]
        for j in range(1, chips):
            leaving = pair[j * rows : (j + 1) * rows].astype(bf16)
            mine = mine + lax.ppermute(leaving, "exp", shift(exp_count, exp_count - 2 * j)).astype(f32)
        if k:
            mine = lax.ppermute(mine.astype(bf16), "seq", shift(seq_count, seq_count - k)).astype(f32)
        total = mine if total is None else total + mine
    return total


def per_device(
    residual,
    mixer_input,
    step_raw,
    state_maps,
    decay_rate,
    skip_gain,
    out_weight,
    norm_gain,
    router_weight,
    expert_ids,
    gate_weight,
    up_weight,
    down_weight,
):
    experts = router_weight.shape[1]
    router = jnp.pad(router_weight, ((0, 0), (0, 128 - experts)))
    skip_gain, router, expert_ids = lax.optimization_barrier((skip_gain, router, expert_ids))
    mixed, blocks = mix(mixer_input, step_raw, state_maps, decay_rate, skip_gain, out_weight)
    weights = (gate_weight, up_weight, down_weight)
    held = [hold(weight, mixed) for weight in weights]
    order = [0] + [block[0] for block in blocks]
    pieces = [(out_weight,)] + [block[1:] for block in blocks]
    sets = []
    for part in (slice(0, -1), slice(-1, None)):
        keep, away = project(mixed, pieces[part])
        sets.append((order[part], sum_to_owner(keep, away)))
    stream, packed = route(sets, residual, norm_gain, router, experts, expert_ids)
    capacity = max(2, 8 * residual.shape[0] // (3 * experts))
    added = experts_sum(packed, experts, capacity, *held)
    return (stream.astype(f32) + added).astype(bf16)


def solution(mesh):
    in_specs = (
        P(("groups", "seq", "exp"), None),
        P(None, ("groups", "seq"), "exp"),
        P(("groups", "seq"), "exp"),
        P(None, None, ("groups", "seq")),
        P(None, "exp"),
        P("exp"),
        P("exp", "seq"),
        P(),
        P(),
        P(("groups", "seq", "exp"), None),
        P("exp", None, "seq"),
        P("exp", None, "seq"),
        P("exp", "seq", None),
    )
    out_specs = P(("groups", "seq", "exp"), None)

    return jax.shard_map(per_device, mesh=mesh, in_specs=in_specs, out_specs=out_specs, check_vma=False)
```

```python
import functools

import jax
import jax.numpy as jnp
from jax import lax
from jax.experimental import pallas as pl
from jax.experimental.pallas import tpu as pltpu
from jax.sharding import PartitionSpec as P

LOG2E = 1.4426950408889634
f32 = jnp.float32
bf16 = jnp.bfloat16
VMEM_EXPERT = 16
VMEM = pl.BlockSpec(memory_space=pltpu.VMEM)
SMEM = pl.BlockSpec(memory_space=pltpu.SMEM)


def softplus(v):
    return jnp.maximum(v, 0.0) + jnp.log1p(jnp.exp(-jnp.abs(v)))


def load_decay(rate_ref, dec_ref):
    states, groups = dec_ref.shape[0] * 128 // rate_ref.shape[1], rate_ref.shape[1] // 128
    for g in range(groups):
        lanes = slice(g * 128, (g + 1) * 128)
        dec_ref[pl.ds(g, states, stride=groups), :] = -LOG2E * rate_ref[:, lanes]


def ends_kernel(maps_ref, raw_ref, mixer_ref, rate_ref, pack_ref, step_ref, drive_ref, dec_ref):
    rows, channels = raw_ref.shape
    groups = channels // 128
    states = rate_ref.shape[0]
    half = rows // 2
    load_decay(rate_ref, dec_ref)
    dec = [dec_ref[pl.ds(n * groups, groups), :] for n in range(states)]

    @pl.loop(0, rows // 16)
    def _(t):
        for g in range(groups):
            lanes = slice(g * 128, (g + 1) * 128)
            at = pl.ds(t * 16, 16)
            step = softplus(raw_ref[at, lanes].astype(f32))
            to = pl.ds(t * 16 * groups + g, 16, stride=groups)
            step_ref[to, :] = step
            drive_ref[to, :] = step * mixer_ref[0, at, lanes].astype(f32)

    def advance(p, carry):
        total, state = list(carry[0]), [list(v) for v in carry[1]]
        for b in range(2):
            pos = b * half + p
            step = step_ref[pl.ds(pos * groups, groups), :]
            drive = drive_ref[pl.ds(pos * groups, groups), :]
            total[b] = total[b] + step
            for n in range(states):
                decay = jnp.exp2(step * dec[n])
                state[b][n] = decay * state[b][n] + drive * maps_ref[n, pos]
        return tuple(total), tuple(tuple(v) for v in state)

    zero = jnp.zeros((groups, 128), f32)
    total, state = lax.fori_loop(
        0, half, advance, ((zero,) * 2, ((zero,) * states,) * 2), unroll=4
    )
    per = 16 // groups
    for b in range(2):
        for n in range(0, states, per):
            values = jnp.concatenate(state[b][n : n + per], axis=0)
            pack_ref[b, pl.ds(n * groups, 16), :] = values.astype(bf16)
        high = total[b].astype(bf16)
        low = (total[b] - high.astype(f32)).astype(bf16)
        pack_ref[b, pl.ds(states * groups, groups), :] = high
        pack_ref[b, pl.ds((states + 1) * groups, groups), :] = low


def scan_kernel(count, maps_ref, step_ref, drive_ref, rate_ref, mixer_ref, skip_ref, *rest):
    packs, (out_ref, all_ref, y_ref, dec_ref) = rest[:count], rest[count:]
    rows, channels = out_ref.shape
    groups = channels // 128
    states = rate_ref.shape[0]
    load_decay(rate_ref, dec_ref)
    dec = [dec_ref[pl.ds(n * groups, groups), :] for n in range(states)]
    half = rows // 2
    place = lax.axis_index("seq")
    for k in range(count):
        all_ref[k] = packs[k][...].astype(f32)

    def fold(b, carry):
        running, first, second = carry
        opening = b < count
        owner = jnp.where(opening, b, 2 * count - 1 - b)
        slot = lax.rem(place - owner + count, count)
        side = jnp.where(opening, 0, 1)
        total = (
            all_ref[slot, side, pl.ds(states * groups, groups), :]
            + all_ref[slot, side, pl.ds((states + 1) * groups, groups), :]
        )
        first = [jnp.where(b == place, r, f) for r, f in zip(running, first)]
        second = [jnp.where(b == 2 * count - 1 - place, r, s) for r, s in zip(running, second)]
        running = [
            jnp.exp2(total * dec[n]) * running[n]
            + all_ref[slot, side, pl.ds(n * groups, groups), :]
            for n in range(states)
        ]
        return running, first, second

    zeros = [all_ref[0, 0, pl.ds(0, groups), :] * 0.0] * states
    _, first, second = lax.fori_loop(0, 2 * count, fold, (zeros, zeros, zeros))

    def advance(p, state):
        state = [list(v) for v in state]
        for b in range(2):
            pos = b * half + p
            at = pl.ds(pos * groups, groups)
            step = step_ref[at, :]
            drive = drive_ref[at, :]
            parts = [None, None]
            for n in range(states):
                decay = jnp.exp2(step * dec[n])
                state[b][n] = decay * state[b][n] + drive * maps_ref[n, pos]
                term = state[b][n] * maps_ref[states + n, pos]
                parts[n % 2] = term if parts[n % 2] is None else parts[n % 2] + term
            y_ref[at, :] = parts[0] + parts[1]
        return tuple(tuple(v) for v in state)

    lax.fori_loop(0, half, advance, (tuple(first), tuple(second)), unroll=4)

    @pl.loop(0, rows // 16)
    def _(t):
        for g in range(groups):
            lanes = slice(g * 128, (g + 1) * 128)
            at = pl.ds(t * 16, 16)
            y = y_ref[pl.ds(t * 16 * groups + g, 16, stride=groups), :]
            x = mixer_ref[0, at, lanes].astype(f32)
            z = mixer_ref[1, at, lanes].astype(f32)
            out_ref[at, lanes] = ((y + skip_ref[:, lanes] * x) * (z * jax.nn.sigmoid(z))).astype(bf16)


def shift(count, k):
    return [(i, (i + k) % count) for i in range(count)]


def after(values, ready):
    return lax.optimization_barrier((values, ready))[0]


def ring_order(count):
    return list(range(1, count // 2 + 1)) + list(range(count - 1, count // 2, -1))


def carrier(count, k):
    return (k - 1, 1) if k <= count // 2 else ((k + 1) % count, count - 1)


def mix(mixer_input, step_raw, state_maps, decay_rate, skip_gain, out_weight):
    rows, channels = step_raw.shape
    groups = channels // 128
    states = decay_rate.shape[0]
    seq_count = lax.axis_size("seq")
    order = ring_order(seq_count)
    swap = [(0, 1), (1, 0)]
    half = out_weight.shape[0] // 2
    group = lax.axis_index("groups")
    mine = lax.dynamic_slice_in_dim(out_weight, group * half, half, 0)
    extra = lax.dynamic_slice_in_dim(out_weight, (1 - group) * half, half // 2, 0)
    direct = {1: lax.ppermute(mine, "seq", shift(seq_count, 1))}

    maps = state_maps.reshape(2 * states, rows).astype(f32)
    shape = jax.ShapeDtypeStruct
    pack, step, drive = pl.pallas_call(
        ends_kernel,
        out_shape=(
            shape((2, (states + 2) * groups, 128), bf16),
            shape((rows * groups, 128), f32),
            shape((rows * groups, 128), f32),
        ),
        in_specs=[SMEM] + [VMEM] * 3,
        out_specs=(VMEM,) * 3,
        scratch_shapes=[pltpu.VMEM((states * groups, 128), f32)],
        compiler_params=pltpu.CompilerParams(vmem_limit_bytes=8 << 20),
        name="ends",
    )(maps, step_raw, mixer_input, decay_rate)
    packs = {0: pack}
    for k in range(1, seq_count):
        packs[k] = lax.ppermute(pack, "seq", shift(seq_count, k))
    packs = [packs[k] for k in range(seq_count)]

    direct[0], direct[1], extra = after((mine, direct[1], extra), packs)
    for k in order[1:]:
        source, step_size = carrier(seq_count, k)
        direct[k] = lax.ppermute(direct[source], "seq", shift(seq_count, step_size))
    last = order[-1]
    direct_more = lax.ppermute(extra, "seq", shift(seq_count, last))
    blocks = []
    for k in order[:-1]:
        other = lax.ppermute(direct[k], "groups", swap)
        blocks.append((k, ((1, 0, direct[k]), (2, 0, other))))
    other = lax.ppermute(direct[last][half // 2 :], "groups", swap)
    blocks.append((last, ((1, 0, direct[last]), (2, 0, direct_more), (2, half // 2, other))))

    mixed = pl.pallas_call(
        functools.partial(scan_kernel, seq_count),
        out_shape=shape((rows, channels), bf16),
        in_specs=[SMEM] + [VMEM] * (5 + seq_count),
        out_specs=VMEM,
        scratch_shapes=[
            pltpu.VMEM((seq_count, 2, (states + 2) * groups, 128), f32),
            pltpu.VMEM((rows * groups, 128), f32),
            pltpu.VMEM((states * groups, 128), f32),
        ],
        compiler_params=pltpu.CompilerParams(vmem_limit_bytes=12 << 20),
        name="scan",
    )(maps, step, drive, decay_rate, mixer_input, skip_gain[None, :], *packs)
    return mixed, blocks


def project_kernel(kinds, mixed_ref, *refs):
    keep_ref, away_ref = refs[-2:]
    core = lax.rem(lax.axis_index("exp"), 2)
    group = lax.axis_index("groups")
    chips = lax.axis_size("exp") // 2
    rows = mixed_ref.shape[0] // (2 * chips)
    half = mixed_ref.shape[1] // 2
    spans = (
        slice(None),
        pl.ds(pl.multiple_of(group * half, 128), half),
        pl.ds(pl.multiple_of((1 - group) * half, 128), half),
    )
    for to_ref, side in ((keep_ref, core), (away_ref, 1 - core)):
        parts = [
            jnp.concatenate(
                [mixed_ref[pl.ds(pl.multiple_of((2 * x + side) * rows, rows), rows), span] for x in range(chips)],
                axis=0,
            )
            for span in spans
        ]
        at = 0
        used = 0
        for piece in kinds:
            width = refs[used].shape[1]
            value = None
            for which, start in piece:
                depth = refs[used].shape[0]
                term = jnp.dot(
                    parts[which][:, start : start + depth], refs[used][...], preferred_element_type=f32
                )
                value = term if value is None else value + term
                used += 1
            to_ref[:, at : at + width] = value
            at += width


def project(mixed, pieces):
    kinds = tuple(tuple(part[:2] for part in piece) for piece in pieces)
    arrays = [part[2] for piece in pieces for part in piece]
    width = sum(piece[0][2].shape[1] for piece in pieces)
    out = jax.ShapeDtypeStruct((mixed.shape[0] // 2, width), f32)
    return pl.pallas_call(
        functools.partial(project_kernel, kinds),
        out_shape=(out, out),
        in_specs=[VMEM] * (1 + len(arrays)),
        out_specs=(VMEM, VMEM),
        compiler_params=pltpu.CompilerParams(vmem_limit_bytes=12 << 20),
        cost_estimate=pl.CostEstimate(
            flops=2 * mixed.size * width, bytes_accessed=2 * mixed.shape[1] * width, transcendentals=0
        ),
        name="project",
    )(mixed, *arrays)


def leave_kernel(keep_ref, theirs_ref, *out_refs):
    chips = len(out_refs) + 1
    chip = lax.axis_index("exp") // 2
    rows = keep_ref.shape[0] // chips
    for j in range(1, chips):
        at = pl.ds(pl.multiple_of(lax.rem(chip + j, chips) * rows, rows), rows)
        out_refs[j - 1][...] = (keep_ref[at, :] + theirs_ref[at, :]).astype(bf16)


def sum_to_owner(keep, away):
    exp_count = lax.axis_size("exp")
    chips = exp_count // 2
    theirs = lax.ppermute(away, "exp", [(i, i ^ 1) for i in range(exp_count)])
    terms = [keep, theirs]
    out = jax.ShapeDtypeStruct((keep.shape[0] // chips, keep.shape[1]), bf16)
    leaving = pl.pallas_call(
        leave_kernel,
        out_shape=(out,) * (chips - 1),
        in_specs=[VMEM] * 2,
        out_specs=(VMEM,) * (chips - 1),
        compiler_params=pltpu.CompilerParams(vmem_limit_bytes=8 << 20),
        name="leave",
    )(keep, theirs)
    for j in range(1, chips):
        terms.append(lax.ppermute(leaving[j - 1], "exp", shift(exp_count, 2 * j)))
    return terms


def route_kernel(sets, experts, *refs):
    count = sum(len(ks) for ks, _ in sets)
    terms_total = sum(terms for _, terms in sets)
    terms, (residual_ref, gain_ref, router_ref, ids_ref) = refs[:terms_total], refs[terms_total : terms_total + 4]
    stream_ref, packed_ref, sum_ref = refs[terms_total + 4 :]
    rows, width = residual_ref.shape
    part = width // count
    place = lax.axis_index("seq")
    mine = pl.ds(pl.multiple_of(lax.axis_index("exp") // 2 * rows, rows), rows)
    used = 0
    for ks, number in sets:
        for i, k in enumerate(ks):
            lanes = slice(i * part, (i + 1) * part)
            value = terms[used][mine, lanes] + terms[used + 1][mine, lanes]
            for extra in range(2, number):
                value = value + terms[used + extra][:, lanes].astype(f32)
            at = pl.multiple_of(lax.rem(place - k + count, count) * part, 128)
            sum_ref[:, pl.ds(at, part)] = value
        used += number
    stream = (residual_ref[...].astype(f32) + sum_ref[...]).astype(bf16)
    stream_ref[...] = stream
    stream = stream.astype(f32)
    mean_sq = jnp.mean(stream * stream, axis=1, keepdims=True)
    normed = (stream * lax.rsqrt(mean_sq + 1e-05) * gain_ref[...]).astype(bf16)
    packed_ref[:, :width] = normed
    lane = lax.broadcasted_iota(jnp.int32, (rows, 128), 1)
    logits = jnp.zeros((rows, 128), f32)
    for e in range(experts):
        product = normed.astype(f32) * router_ref[e : e + 1, :].astype(f32)
        logits = jnp.where(lane == e, jnp.sum(product, axis=1, keepdims=True), logits)
    row, column = (lax.broadcasted_iota(jnp.int32, (rows, rows), d) for d in range(2))
    same = jnp.where(row == column, 1.0, 0.0).astype(bf16)
    name = lax.broadcasted_iota(jnp.int32, (128, rows), 0)

    def picked(choice):
        hot = jnp.where(ids_ref[choice : choice + 1, :] == name, 1.0, 0.0).astype(bf16)
        return lax.dot_general(same, hot, (((1,), (1,)), ((), ())), preferred_element_type=f32) > 0.5

    first, second = picked(0), picked(1)
    gap = jnp.sum(jnp.where(first, logits, 0.0), axis=1, keepdims=True) - jnp.sum(
        jnp.where(second, logits, 0.0), axis=1, keepdims=True
    )
    weight = jnp.where(first, jax.nn.sigmoid(gap), 0.0) + jnp.where(second, jax.nn.sigmoid(-gap), 0.0)
    routed = jnp.where(first, 1.0, 0.0) + jnp.where(second, 1.0, 0.0)
    earlier = jnp.where(row > column, 1.0, 0.0)
    slot = jnp.dot(earlier.astype(bf16), routed.astype(bf16), preferred_element_type=f32)
    slot = jnp.where(routed > 0.0, slot + 1.0, 0.0)
    high = weight.astype(bf16).astype(f32)
    lanes = high + pltpu.roll(weight - high, experts, 1) + pltpu.roll(slot, 2 * experts, 1)
    packed_ref[:, width:] = lanes.astype(bf16)


def route(sets, residual, norm_gain, router_weight, expert_ids):
    rows, width = residual.shape
    experts = router_weight.shape[1]
    shape = jax.ShapeDtypeStruct
    terms = [term for _, group in sets for term in group]
    kinds = tuple((tuple(ks), len(group)) for ks, group in sets)
    return pl.pallas_call(
        functools.partial(route_kernel, kinds, experts),
        out_shape=(shape((rows, width), bf16), shape((rows, width + 128), bf16)),
        in_specs=[VMEM] * (len(terms) + 4),
        out_specs=(VMEM, VMEM),
        scratch_shapes=[pltpu.VMEM((rows, width), f32)],
        compiler_params=pltpu.CompilerParams(vmem_limit_bytes=8 << 20),
        name="route",
    )(*terms, residual, norm_gain[None, :], router_weight.T, expert_ids.T)


def expert_kernel(capacity, block_rows, experts, tile, own_ref, mate_ref, gate_ref, up_ref, down_ref, *rest):
    keep_ref, send_ref, acc_ref = rest
    rows, width = keep_ref.shape
    slots = acc_ref.shape[0]
    lane = lax.broadcasted_iota(jnp.int32, (1, 128), 1)
    place = lax.axis_index("exp")
    picked = lane == 2 * experts + place
    wanted = jnp.broadcast_to(jnp.where(picked, 1.0, 0.0), (8, 128)).astype(bf16)
    held = None
    for side, ref in enumerate((own_ref, mate_ref)):
        slot = lax.dot_general(
            wanted, ref[:, width:], (((1,), (1,)), ((), ())), preferred_element_type=f32
        )[0:1, :].astype(jnp.int32)
        block = lax.broadcasted_iota(jnp.int32, (1, rows), 1) // block_rows + side * (rows // block_rows)
        target = jnp.where(slot > 0, block * capacity + slot - 1, -1)
        chosen = jnp.where(lax.broadcasted_iota(jnp.int32, (slots, rows), 0) == target, 1.0, 0.0)
        value = jnp.dot(chosen.astype(bf16), ref[...], preferred_element_type=f32)
        held = value if held is None else held + value
    mine = (lane == place) | (lane == experts + place)
    weight = jnp.sum(jnp.where(mine, held[:, width:], 0.0), axis=1, keepdims=True)
    held = held[:, :width].astype(bf16)

    for t in range(gate_ref.shape[2] // tile):
        at = slice(t * tile, (t + 1) * tile)
        gated = jnp.dot(held, gate_ref[0, :, at], preferred_element_type=f32)
        upper = jnp.dot(held, up_ref[0, :, at], preferred_element_type=f32)
        hidden = (gated * jax.nn.sigmoid(gated) * upper).astype(bf16)
        value = jnp.dot(hidden, down_ref[0, at, :], preferred_element_type=f32)
        if t == 0:
            acc_ref[...] = value
        else:
            acc_ref[...] += value

    scaled = (acc_ref[...] * weight).astype(bf16)
    for side, ref in enumerate((own_ref, mate_ref)):
        slot = jnp.sum(jnp.where(picked, ref[:, width:].astype(f32), 0.0), axis=1, keepdims=True)
        block = lax.broadcasted_iota(jnp.int32, (rows, 1), 0) // block_rows + side * (rows // block_rows)
        target = jnp.where(slot > 0.0, block * capacity + slot.astype(jnp.int32) - 1, -1)
        chosen = jnp.where(lax.broadcasted_iota(jnp.int32, (rows, slots), 1) == target, 1.0, 0.0)
        back = jnp.dot(chosen.astype(bf16), scaled, preferred_element_type=f32)
        if side == 0:
            keep_ref[...] = back
        else:
            send_ref[...] = back.astype(bf16)


def hold_kernel(from_ref, to_ref):
    pltpu.sync_copy(from_ref, to_ref)


def hold(weight, ready):
    return pl.pallas_call(
        hold_kernel,
        out_shape=jax.ShapeDtypeStruct(weight.shape, weight.dtype),
        in_specs=[pl.BlockSpec(memory_space=pl.ANY)],
        out_specs=VMEM,
        compiler_params=pltpu.CompilerParams(vmem_limit_bytes=16 << 20),
        cost_estimate=pl.CostEstimate(flops=0, bytes_accessed=2 * weight.size, transcendentals=0),
        name="hold",
    )(after(weight, ready))


def expert_part(own, mate, capacity, block_rows, experts, gate, up, down):
    rows, width = own.shape[0], own.shape[1] - 128
    hidden = gate.shape[2]
    tile = 256 if hidden % 256 == 0 else hidden
    slots = -(-2 * rows // block_rows * capacity // 16) * 16
    shape = jax.ShapeDtypeStruct
    return pl.pallas_call(
        functools.partial(expert_kernel, capacity, block_rows, experts, tile),
        out_shape=(shape((rows, width), f32), shape((rows, width), bf16)),
        in_specs=[VMEM] * 5,
        out_specs=(VMEM, VMEM),
        scratch_shapes=[pltpu.VMEM((slots, width), f32)],
        compiler_params=pltpu.CompilerParams(vmem_limit_bytes=VMEM_EXPERT << 20),
        cost_estimate=pl.CostEstimate(
            flops=6 * slots * width * hidden,
            bytes_accessed=6 * width * hidden,
            transcendentals=slots * hidden,
        ),
        name="expert",
    )(own, mate, gate, up, down)


def experts_sum(packed, experts, capacity, gate, up, down):
    seq_count = lax.axis_size("seq")
    exp_count = lax.axis_size("exp")
    chips = exp_count // 2
    rows = packed.shape[0]
    partner = [(i, i ^ 1) for i in range(exp_count)]
    order = ring_order(seq_count)

    planes = {0: packed}
    for k in order:
        source, step_size = carrier(seq_count, k)
        planes[k] = lax.ppermute(planes[source], "seq", shift(seq_count, step_size))

    total = None
    for k in [0] + order:
        row = [planes[k]]
        for j in range(1, chips):
            row.append(lax.ppermute(planes[k], "exp", shift(exp_count, 2 * j)))
        row = jnp.concatenate(row, axis=0)
        mate = lax.ppermute(row, "exp", partner)
        keep, send = expert_part(row, mate, capacity, rows, experts, gate, up, down)
        pair = keep + lax.ppermute(send, "exp", partner).astype(f32)
        mine = pair[:rows]
        for j in range(1, chips):
            leaving = pair[j * rows : (j + 1) * rows].astype(bf16)
            mine = mine + lax.ppermute(leaving, "exp", shift(exp_count, exp_count - 2 * j)).astype(f32)
        if k:
            mine = lax.ppermute(mine.astype(bf16), "seq", shift(seq_count, seq_count - k)).astype(f32)
        total = mine if total is None else total + mine
    return total


def per_device(
    residual,
    mixer_input,
    step_raw,
    state_maps,
    decay_rate,
    skip_gain,
    out_weight,
    norm_gain,
    router_weight,
    expert_ids,
    gate_weight,
    up_weight,
    down_weight,
):
    experts = router_weight.shape[1]
    mixed, blocks = mix(mixer_input, step_raw, state_maps, decay_rate, skip_gain, out_weight)
    weights = (gate_weight, up_weight, down_weight)
    held = [hold(weight, mixed) for weight in weights]
    order = [0] + [block[0] for block in blocks]
    pieces = [((0, 0, out_weight),)] + [block[1] for block in blocks]
    sets = []
    for part in (slice(0, -1), slice(-1, None)):
        keep, away = project(mixed, pieces[part])
        sets.append((order[part], sum_to_owner(keep, away)))
    stream, packed = route(sets, residual, norm_gain, router_weight, expert_ids)
    capacity = max(2, 8 * residual.shape[0] // (3 * experts))
    added = experts_sum(packed, experts, capacity, *held)
    return (stream.astype(f32) + added).astype(bf16)


def solution(mesh):
    in_specs = (
        P(("groups", "seq", "exp"), None),
        P(None, ("groups", "seq"), "exp"),
        P(("groups", "seq"), "exp"),
        P(None, None, ("groups", "seq")),
        P(None, "exp"),
        P("exp"),
        P("exp", "seq"),
        P(),
        P(),
        P(("groups", "seq", "exp"), None),
        P("exp", None, "seq"),
        P("exp", None, "seq"),
        P("exp", "seq", None),
    )
    out_specs = P(("groups", "seq", "exp"), None)

    return jax.shard_map(per_device, mesh=mesh, in_specs=in_specs, out_specs=out_specs, check_vma=False)
```

```python
import functools

import jax
import jax.numpy as jnp
from jax import lax
from jax.experimental import pallas as pl
from jax.experimental.pallas import tpu as pltpu
from jax.sharding import PartitionSpec as P

LOG2E = 1.4426950408889634
f32 = jnp.float32
bf16 = jnp.bfloat16
VMEM_EXPERT = 16
VMEM = pl.BlockSpec(memory_space=pltpu.VMEM)
SMEM = pl.BlockSpec(memory_space=pltpu.SMEM)


def softplus(v):
    return jnp.maximum(v, 0.0) + jnp.log1p(jnp.exp(-jnp.abs(v)))


def load_decay(rate_ref, dec_ref):
    states, groups = dec_ref.shape[0] * 128 // rate_ref.shape[1], rate_ref.shape[1] // 128
    for g in range(groups):
        lanes = slice(g * 128, (g + 1) * 128)
        dec_ref[pl.ds(g, states, stride=groups), :] = -LOG2E * rate_ref[:, lanes]


def ends_kernel(maps_ref, raw_ref, mixer_ref, rate_ref, pack_ref, step_ref, drive_ref, dec_ref):
    rows, channels = raw_ref.shape
    groups = channels // 128
    states = rate_ref.shape[0]
    half = rows // 2
    load_decay(rate_ref, dec_ref)
    dec = [dec_ref[pl.ds(n * groups, groups), :] for n in range(states)]

    @pl.loop(0, rows // 16)
    def _(t):
        for g in range(groups):
            lanes = slice(g * 128, (g + 1) * 128)
            at = pl.ds(t * 16, 16)
            step = softplus(raw_ref[at, lanes].astype(f32))
            to = pl.ds(t * 16 * groups + g, 16, stride=groups)
            step_ref[to, :] = step
            drive_ref[to, :] = step * mixer_ref[0, at, lanes].astype(f32)

    def advance(p, carry):
        total, state = list(carry[0]), [list(v) for v in carry[1]]
        for b in range(2):
            pos = b * half + p
            step = step_ref[pl.ds(pos * groups, groups), :]
            drive = drive_ref[pl.ds(pos * groups, groups), :]
            total[b] = total[b] + step
            for n in range(states):
                decay = jnp.exp2(step * dec[n])
                state[b][n] = decay * state[b][n] + drive * maps_ref[n, pos]
        return tuple(total), tuple(tuple(v) for v in state)

    zero = jnp.zeros((groups, 128), f32)
    total, state = lax.fori_loop(
        0, half, advance, ((zero,) * 2, ((zero,) * states,) * 2), unroll=4
    )
    per = 16 // groups
    for b in range(2):
        for n in range(0, states, per):
            values = jnp.concatenate(state[b][n : n + per], axis=0)
            pack_ref[b, pl.ds(n * groups, 16), :] = values.astype(bf16)
        high = total[b].astype(bf16)
        low = (total[b] - high.astype(f32)).astype(bf16)
        pack_ref[b, pl.ds(states * groups, groups), :] = high
        pack_ref[b, pl.ds((states + 1) * groups, groups), :] = low


def scan_kernel(count, maps_ref, step_ref, drive_ref, rate_ref, mixer_ref, skip_ref, *rest):
    packs, (out_ref, all_ref, y_ref, dec_ref) = rest[:count], rest[count:]
    rows, channels = out_ref.shape
    groups = channels // 128
    states = rate_ref.shape[0]
    load_decay(rate_ref, dec_ref)
    dec = [dec_ref[pl.ds(n * groups, groups), :] for n in range(states)]
    half = rows // 2
    place = lax.axis_index("seq")
    for k in range(count):
        all_ref[k] = packs[k][...].astype(f32)

    def fold(b, carry):
        running, first, second = carry
        opening = b < count
        owner = jnp.where(opening, b, 2 * count - 1 - b)
        slot = lax.rem(place - owner + count, count)
        side = jnp.where(opening, 0, 1)
        total = (
            all_ref[slot, side, pl.ds(states * groups, groups), :]
            + all_ref[slot, side, pl.ds((states + 1) * groups, groups), :]
        )
        first = [jnp.where(b == place, r, f) for r, f in zip(running, first)]
        second = [jnp.where(b == 2 * count - 1 - place, r, s) for r, s in zip(running, second)]
        running = [
            jnp.exp2(total * dec[n]) * running[n]
            + all_ref[slot, side, pl.ds(n * groups, groups), :]
            for n in range(states)
        ]
        return running, first, second

    zeros = [all_ref[0, 0, pl.ds(0, groups), :] * 0.0] * states
    _, first, second = lax.fori_loop(0, 2 * count, fold, (zeros, zeros, zeros))

    def advance(p, state):
        state = [list(v) for v in state]
        for b in range(2):
            pos = b * half + p
            at = pl.ds(pos * groups, groups)
            step = step_ref[at, :]
            drive = drive_ref[at, :]
            parts = [None, None]
            for n in range(states):
                decay = jnp.exp2(step * dec[n])
                state[b][n] = decay * state[b][n] + drive * maps_ref[n, pos]
                term = state[b][n] * maps_ref[states + n, pos]
                parts[n % 2] = term if parts[n % 2] is None else parts[n % 2] + term
            y_ref[at, :] = parts[0] + parts[1]
        return tuple(tuple(v) for v in state)

    lax.fori_loop(0, half, advance, (tuple(first), tuple(second)), unroll=4)

    @pl.loop(0, rows // 16)
    def _(t):
        for g in range(groups):
            lanes = slice(g * 128, (g + 1) * 128)
            at = pl.ds(t * 16, 16)
            y = y_ref[pl.ds(t * 16 * groups + g, 16, stride=groups), :]
            x = mixer_ref[0, at, lanes].astype(f32)
            z = mixer_ref[1, at, lanes].astype(f32)
            out_ref[at, lanes] = ((y + skip_ref[:, lanes] * x) * (z * jax.nn.sigmoid(z))).astype(bf16)


def shift(count, k):
    return [(i, (i + k) % count) for i in range(count)]


def after(values, ready):
    return lax.optimization_barrier((values, ready))[0]


def ring_order(count):
    return list(range(1, count // 2 + 1)) + list(range(count - 1, count // 2, -1))


def carrier(count, k):
    return (k - 1, 1) if k <= count // 2 else ((k + 1) % count, count - 1)


def pick_kernel(from_ref, mine_ref, extra_ref, sems):
    half, more = mine_ref.shape[0], extra_ref.shape[0]
    group = lax.axis_index("groups")
    own = pl.ds(pl.multiple_of(group * half, 16), half)
    next_rows = pl.ds(pl.multiple_of((1 - group) * half, 16), more)
    copies = [
        pltpu.make_async_copy(from_ref.at[own, :], mine_ref, sems.at[0]),
        pltpu.make_async_copy(from_ref.at[next_rows, :], extra_ref, sems.at[1]),
    ]
    for copy in copies:
        copy.start()
    for copy in copies:
        copy.wait()


def pick_rows(out_weight):
    rows, width = out_weight.shape
    shape = jax.ShapeDtypeStruct
    return pl.pallas_call(
        pick_kernel,
        out_shape=(shape((rows // 2, width), bf16), shape((rows // 4, width), bf16)),
        in_specs=[pl.BlockSpec(memory_space=pl.ANY)],
        out_specs=(VMEM, VMEM),
        scratch_shapes=[pltpu.SemaphoreType.DMA((2,))],
        compiler_params=pltpu.CompilerParams(vmem_limit_bytes=4 << 20),
        name="pick",
    )(out_weight)


def mix(mixer_input, step_raw, state_maps, decay_rate, skip_gain, out_weight):
    rows, channels = step_raw.shape
    groups = channels // 128
    states = decay_rate.shape[0]
    seq_count = lax.axis_size("seq")
    order = ring_order(seq_count)
    swap = [(0, 1), (1, 0)]
    half = out_weight.shape[0] // 2
    mine, extra = pick_rows(out_weight)
    direct = {1: lax.ppermute(mine, "seq", shift(seq_count, 1))}

    maps = state_maps.reshape(2 * states, rows).astype(f32)
    shape = jax.ShapeDtypeStruct
    pack, step, drive = pl.pallas_call(
        ends_kernel,
        out_shape=(
            shape((2, (states + 2) * groups, 128), bf16),
            shape((rows * groups, 128), f32),
            shape((rows * groups, 128), f32),
        ),
        in_specs=[SMEM] + [VMEM] * 3,
        out_specs=(VMEM,) * 3,
        scratch_shapes=[pltpu.VMEM((states * groups, 128), f32)],
        compiler_params=pltpu.CompilerParams(vmem_limit_bytes=8 << 20),
        name="ends",
    )(maps, step_raw, mixer_input, decay_rate)
    packs = {0: pack}
    for k in range(1, seq_count):
        packs[k] = lax.ppermute(pack, "seq", shift(seq_count, k))
    packs = [packs[k] for k in range(seq_count)]

    direct[0], direct[1], extra = after((mine, direct[1], extra), packs)
    for k in order[1:]:
        source, step_size = carrier(seq_count, k)
        direct[k] = lax.ppermute(direct[source], "seq", shift(seq_count, step_size))
    last = order[-1]
    direct_more = lax.ppermute(extra, "seq", shift(seq_count, last))
    blocks = []
    for k in order[:-1]:
        other = lax.ppermute(direct[k], "groups", swap)
        blocks.append((k, ((1, 0, direct[k]), (2, 0, other))))
    other = lax.ppermute(direct[last][half // 2 :], "groups", swap)
    blocks.append((last, ((1, 0, direct[last]), (2, 0, direct_more), (2, half // 2, other))))

    mixed = pl.pallas_call(
        functools.partial(scan_kernel, seq_count),
        out_shape=shape((rows, channels), bf16),
        in_specs=[SMEM] + [VMEM] * (5 + seq_count),
        out_specs=VMEM,
        scratch_shapes=[
            pltpu.VMEM((seq_count, 2, (states + 2) * groups, 128), f32),
            pltpu.VMEM((rows * groups, 128), f32),
            pltpu.VMEM((states * groups, 128), f32),
        ],
        compiler_params=pltpu.CompilerParams(vmem_limit_bytes=12 << 20),
        name="scan",
    )(maps, step, drive, decay_rate, mixer_input, skip_gain[None, :], *packs)
    return mixed, blocks


def project_kernel(kinds, mixed_ref, *refs):
    keep_ref, away_ref = refs[-2:]
    core = lax.rem(lax.axis_index("exp"), 2)
    group = lax.axis_index("groups")
    chips = lax.axis_size("exp") // 2
    rows = mixed_ref.shape[0] // (2 * chips)
    half = mixed_ref.shape[1] // 2
    spans = (
        slice(None),
        pl.ds(pl.multiple_of(group * half, 128), half),
        pl.ds(pl.multiple_of((1 - group) * half, 128), half),
    )
    for to_ref, side in ((keep_ref, core), (away_ref, 1 - core)):
        parts = [
            jnp.concatenate(
                [mixed_ref[pl.ds(pl.multiple_of((2 * x + side) * rows, rows), rows), span] for x in range(chips)],
                axis=0,
            )
            for span in spans
        ]
        at = 0
        used = 0
        for piece in kinds:
            width = refs[used].shape[1]
            value = None
            for which, start in piece:
                depth = refs[used].shape[0]
                term = jnp.dot(
                    parts[which][:, start : start + depth], refs[used][...], preferred_element_type=f32
                )
                value = term if value is None else value + term
                used += 1
            to_ref[:, at : at + width] = value
            at += width


def project(mixed, pieces):
    kinds = tuple(tuple(part[:2] for part in piece) for piece in pieces)
    arrays = [part[2] for piece in pieces for part in piece]
    width = sum(piece[0][2].shape[1] for piece in pieces)
    out = jax.ShapeDtypeStruct((mixed.shape[0] // 2, width), f32)
    return pl.pallas_call(
        functools.partial(project_kernel, kinds),
        out_shape=(out, out),
        in_specs=[VMEM] * (1 + len(arrays)),
        out_specs=(VMEM, VMEM),
        compiler_params=pltpu.CompilerParams(vmem_limit_bytes=12 << 20),
        cost_estimate=pl.CostEstimate(
            flops=2 * mixed.size * width, bytes_accessed=2 * mixed.shape[1] * width, transcendentals=0
        ),
        name="project",
    )(mixed, *arrays)


def leave_kernel(keep_ref, theirs_ref, *out_refs):
    chips = len(out_refs) + 1
    chip = lax.axis_index("exp") // 2
    rows = keep_ref.shape[0] // chips
    for j in range(1, chips):
        at = pl.ds(pl.multiple_of(lax.rem(chip + j, chips) * rows, rows), rows)
        out_refs[j - 1][...] = (keep_ref[at, :] + theirs_ref[at, :]).astype(bf16)


def sum_to_owner(keep, away):
    exp_count = lax.axis_size("exp")
    chips = exp_count // 2
    theirs = lax.ppermute(away, "exp", [(i, i ^ 1) for i in range(exp_count)])
    terms = [keep, theirs]
    out = jax.ShapeDtypeStruct((keep.shape[0] // chips, keep.shape[1]), bf16)
    leaving = pl.pallas_call(
        leave_kernel,
        out_shape=(out,) * (chips - 1),
        in_specs=[VMEM] * 2,
        out_specs=(VMEM,) * (chips - 1),
        compiler_params=pltpu.CompilerParams(vmem_limit_bytes=8 << 20),
        name="leave",
    )(keep, theirs)
    for j in range(1, chips):
        terms.append(lax.ppermute(leaving[j - 1], "exp", shift(exp_count, 2 * j)))
    return terms


def route_kernel(sets, experts, *refs):
    count = sum(len(ks) for ks, _ in sets)
    terms_total = sum(terms for _, terms in sets)
    terms, (residual_ref, gain_ref, router_ref, ids_ref) = refs[:terms_total], refs[terms_total : terms_total + 4]
    stream_ref, packed_ref, sum_ref = refs[terms_total + 4 :]
    rows, width = residual_ref.shape
    part = width // count
    place = lax.axis_index("seq")
    mine = pl.ds(pl.multiple_of(lax.axis_index("exp") // 2 * rows, rows), rows)
    used = 0
    for ks, number in sets:
        for i, k in enumerate(ks):
            lanes = slice(i * part, (i + 1) * part)
            value = terms[used][mine, lanes] + terms[used + 1][mine, lanes]
            for extra in range(2, number):
                value = value + terms[used + extra][:, lanes].astype(f32)
            at = pl.multiple_of(lax.rem(place - k + count, count) * part, 128)
            sum_ref[:, pl.ds(at, part)] = value
        used += number
    stream = (residual_ref[...].astype(f32) + sum_ref[...]).astype(bf16)
    stream_ref[...] = stream
    stream = stream.astype(f32)
    mean_sq = jnp.mean(stream * stream, axis=1, keepdims=True)
    normed = (stream * lax.rsqrt(mean_sq + 1e-05) * gain_ref[...]).astype(bf16)
    packed_ref[:, :width] = normed
    lane = lax.broadcasted_iota(jnp.int32, (rows, 128), 1)
    logits = jnp.zeros((rows, 128), f32)
    for e in range(experts):
        product = normed.astype(f32) * router_ref[e : e + 1, :].astype(f32)
        logits = jnp.where(lane == e, jnp.sum(product, axis=1, keepdims=True), logits)
    row, column = (lax.broadcasted_iota(jnp.int32, (rows, rows), d) for d in range(2))
    same = jnp.where(row == column, 1.0, 0.0).astype(bf16)
    name = lax.broadcasted_iota(jnp.int32, (128, rows), 0)

    def picked(choice):
        hot = jnp.where(ids_ref[choice : choice + 1, :] == name, 1.0, 0.0).astype(bf16)
        return lax.dot_general(same, hot, (((1,), (1,)), ((), ())), preferred_element_type=f32) > 0.5

    first, second = picked(0), picked(1)
    gap = jnp.sum(jnp.where(first, logits, 0.0), axis=1, keepdims=True) - jnp.sum(
        jnp.where(second, logits, 0.0), axis=1, keepdims=True
    )
    weight = jnp.where(first, jax.nn.sigmoid(gap), 0.0) + jnp.where(second, jax.nn.sigmoid(-gap), 0.0)
    routed = jnp.where(first, 1.0, 0.0) + jnp.where(second, 1.0, 0.0)
    earlier = jnp.where(row > column, 1.0, 0.0)
    slot = jnp.dot(earlier.astype(bf16), routed.astype(bf16), preferred_element_type=f32)
    slot = jnp.where(routed > 0.0, slot + 1.0, 0.0)
    high = weight.astype(bf16).astype(f32)
    lanes = high + pltpu.roll(weight - high, experts, 1) + pltpu.roll(slot, 2 * experts, 1)
    packed_ref[:, width:] = lanes.astype(bf16)


def route(sets, residual, norm_gain, router_weight, expert_ids):
    rows, width = residual.shape
    experts = router_weight.shape[1]
    shape = jax.ShapeDtypeStruct
    terms = [term for _, group in sets for term in group]
    kinds = tuple((tuple(ks), len(group)) for ks, group in sets)
    return pl.pallas_call(
        functools.partial(route_kernel, kinds, experts),
        out_shape=(shape((rows, width), bf16), shape((rows, width + 128), bf16)),
        in_specs=[VMEM] * (len(terms) + 4),
        out_specs=(VMEM, VMEM),
        scratch_shapes=[pltpu.VMEM((rows, width), f32)],
        compiler_params=pltpu.CompilerParams(vmem_limit_bytes=8 << 20),
        name="route",
    )(*terms, residual, norm_gain[None, :], router_weight.T, expert_ids.T)


def expert_kernel(capacity, block_rows, experts, tile, own_ref, mate_ref, gate_ref, up_ref, down_ref, *rest):
    keep_ref, send_ref, acc_ref = rest
    rows, width = keep_ref.shape
    slots = acc_ref.shape[0]
    lane = lax.broadcasted_iota(jnp.int32, (1, 128), 1)
    place = lax.axis_index("exp")
    picked = lane == 2 * experts + place
    wanted = jnp.broadcast_to(jnp.where(picked, 1.0, 0.0), (8, 128)).astype(bf16)
    held = None
    for side, ref in enumerate((own_ref, mate_ref)):
        slot = lax.dot_general(
            wanted, ref[:, width:], (((1,), (1,)), ((), ())), preferred_element_type=f32
        )[0:1, :].astype(jnp.int32)
        block = lax.broadcasted_iota(jnp.int32, (1, rows), 1) // block_rows + side * (rows // block_rows)
        target = jnp.where(slot > 0, block * capacity + slot - 1, -1)
        chosen = jnp.where(lax.broadcasted_iota(jnp.int32, (slots, rows), 0) == target, 1.0, 0.0)
        value = jnp.dot(chosen.astype(bf16), ref[...], preferred_element_type=f32)
        held = value if held is None else held + value
    mine = (lane == place) | (lane == experts + place)
    weight = jnp.sum(jnp.where(mine, held[:, width:], 0.0), axis=1, keepdims=True)
    held = held[:, :width].astype(bf16)

    for t in range(gate_ref.shape[2] // tile):
        at = slice(t * tile, (t + 1) * tile)
        gated = jnp.dot(held, gate_ref[0, :, at], preferred_element_type=f32)
        upper = jnp.dot(held, up_ref[0, :, at], preferred_element_type=f32)
        hidden = (gated * jax.nn.sigmoid(gated) * upper).astype(bf16)
        value = jnp.dot(hidden, down_ref[0, at, :], preferred_element_type=f32)
        if t == 0:
            acc_ref[...] = value
        else:
            acc_ref[...] += value

    scaled = (acc_ref[...] * weight).astype(bf16)
    for side, ref in enumerate((own_ref, mate_ref)):
        slot = jnp.sum(jnp.where(picked, ref[:, width:].astype(f32), 0.0), axis=1, keepdims=True)
        block = lax.broadcasted_iota(jnp.int32, (rows, 1), 0) // block_rows + side * (rows // block_rows)
        target = jnp.where(slot > 0.0, block * capacity + slot.astype(jnp.int32) - 1, -1)
        chosen = jnp.where(lax.broadcasted_iota(jnp.int32, (rows, slots), 1) == target, 1.0, 0.0)
        back = jnp.dot(chosen.astype(bf16), scaled, preferred_element_type=f32)
        if side == 0:
            keep_ref[...] = back
        else:
            send_ref[...] = back.astype(bf16)


def hold_kernel(from_ref, to_ref):
    pltpu.sync_copy(from_ref, to_ref)


def hold(weight, ready):
    return pl.pallas_call(
        hold_kernel,
        out_shape=jax.ShapeDtypeStruct(weight.shape, weight.dtype),
        in_specs=[pl.BlockSpec(memory_space=pl.ANY)],
        out_specs=VMEM,
        compiler_params=pltpu.CompilerParams(vmem_limit_bytes=16 << 20),
        cost_estimate=pl.CostEstimate(flops=0, bytes_accessed=2 * weight.size, transcendentals=0),
        name="hold",
    )(after(weight, ready))


def expert_part(own, mate, capacity, block_rows, experts, gate, up, down):
    rows, width = own.shape[0], own.shape[1] - 128
    hidden = gate.shape[2]
    tile = 256 if hidden % 256 == 0 else hidden
    slots = -(-2 * rows // block_rows * capacity // 16) * 16
    shape = jax.ShapeDtypeStruct
    return pl.pallas_call(
        functools.partial(expert_kernel, capacity, block_rows, experts, tile),
        out_shape=(shape((rows, width), f32), shape((rows, width), bf16)),
        in_specs=[VMEM] * 5,
        out_specs=(VMEM, VMEM),
        scratch_shapes=[pltpu.VMEM((slots, width), f32)],
        compiler_params=pltpu.CompilerParams(vmem_limit_bytes=VMEM_EXPERT << 20),
        cost_estimate=pl.CostEstimate(
            flops=6 * slots * width * hidden,
            bytes_accessed=6 * width * hidden,
            transcendentals=slots * hidden,
        ),
        name="expert",
    )(own, mate, gate, up, down)


def experts_sum(packed, experts, capacity, gate, up, down):
    seq_count = lax.axis_size("seq")
    exp_count = lax.axis_size("exp")
    chips = exp_count // 2
    rows = packed.shape[0]
    partner = [(i, i ^ 1) for i in range(exp_count)]
    order = ring_order(seq_count)

    planes = {0: packed}
    for k in order:
        source, step_size = carrier(seq_count, k)
        planes[k] = lax.ppermute(planes[source], "seq", shift(seq_count, step_size))

    total = None
    for k in [0] + order:
        row = [planes[k]]
        for j in range(1, chips):
            row.append(lax.ppermute(planes[k], "exp", shift(exp_count, 2 * j)))
        row = jnp.concatenate(row, axis=0)
        mate = lax.ppermute(row, "exp", partner)
        keep, send = expert_part(row, mate, capacity, rows, experts, gate, up, down)
        pair = keep + lax.ppermute(send, "exp", partner).astype(f32)
        mine = pair[:rows]
        for j in range(1, chips):
            leaving = pair[j * rows : (j + 1) * rows].astype(bf16)
            mine = mine + lax.ppermute(leaving, "exp", shift(exp_count, exp_count - 2 * j)).astype(f32)
        if k:
            mine = lax.ppermute(mine.astype(bf16), "seq", shift(seq_count, seq_count - k)).astype(f32)
        total = mine if total is None else total + mine
    return total


def per_device(
    residual,
    mixer_input,
    step_raw,
    state_maps,
    decay_rate,
    skip_gain,
    out_weight,
    norm_gain,
    router_weight,
    expert_ids,
    gate_weight,
    up_weight,
    down_weight,
):
    experts = router_weight.shape[1]
    mixed, blocks = mix(mixer_input, step_raw, state_maps, decay_rate, skip_gain, out_weight)
    weights = (gate_weight, up_weight, down_weight)
    held = [hold(weight, mixed) for weight in weights]
    order = [0] + [block[0] for block in blocks]
    pieces = [((0, 0, out_weight),)] + [block[1] for block in blocks]
    sets = []
    for part in (slice(0, -1), slice(-1, None)):
        keep, away = project(mixed, pieces[part])
        sets.append((order[part], sum_to_owner(keep, away)))
    stream, packed = route(sets, residual, norm_gain, router_weight, expert_ids)
    capacity = max(2, 8 * residual.shape[0] // (3 * experts))
    added = experts_sum(packed, experts, capacity, *held)
    return (stream.astype(f32) + added).astype(bf16)


def solution(mesh):
    in_specs = (
        P(("groups", "seq", "exp"), None),
        P(None, ("groups", "seq"), "exp"),
        P(("groups", "seq"), "exp"),
        P(None, None, ("groups", "seq")),
        P(None, "exp"),
        P("exp"),
        P("exp", "seq"),
        P(),
        P(),
        P(("groups", "seq", "exp"), None),
        P("exp", None, "seq"),
        P("exp", None, "seq"),
        P("exp", "seq", None),
    )
    out_specs = P(("groups", "seq", "exp"), None)

    return jax.shard_map(per_device, mesh=mesh, in_specs=in_specs, out_specs=out_specs, check_vma=False)
```
